512 devices in a mesh: ka: 16 (over z_hi, x), kp: 32 (over z_lo, y, core).
Axes of the slice: x: 4, y: 4, z: 16 (z_hi: 4, z_lo: 4; z = z_hi * 4 + z_lo), core: 2. Of those that a mesh axis runs over, the one named last changes fastest.
Arguments:
- waves: bfloat16 [32, 16, 4096], P('ka', None, 'kp'), may hold values from -6 to 6
- screen: float32 [32, 512], replicated, may hold values from 0.1 to 2
- pair_table: int32 [32, 32], P('ka', 'kp'), may hold values from 0 to 31
- plane_map: int32 [512], replicated, may hold values from 1 to 4095, as said below
- trial: bfloat16 [32, 64, 128], P('kp', None, 'ka'), may hold values from -6 to 6
- probe: bfloat16 [32, 64, 128], P('ka', None, 'kp'), may hold values from -6 to 6
Outputs:
- applied: float32 [32, 64, 128], P('ka', None, 'kp')
- adjoint: float32 [32, 64, 128], P('kp', None, 'ka')
The draws below stay inside these ranges and needn't reach their ends.
Inputs may be any that keep to these rules, and one draw needn't show every extreme that they name: `plane_map`: the 512 values are distinct and none is 0.
All inputs are finite; a program needn't handle non-finite values.
Results may differ from the reference program's by a relative error of at most 0.0003.
Values may be sent and summed in bfloat16 or wider, within the bound.
No kernel may reach another device: no remote copies, remote signals or barrier semaphores. Data moves between devices by JAX's collectives and lax.ppermute only.
A program may use at most 64 MiB of HBM per device.

```python
import math
import jax
import jax.numpy as jnp
from jax import lax

NV = 8
NC = 8
NR = 4096
NG = 512
M = 128
NK = 32


def draw_plane_map(key, part):
    return (jax.random.permutation(key, NR - 1)[:NG] + 1).astype(jnp.int32)


def place_ends(values, rng, low, top_value):
    spot = [jax.random.randint(jax.random.fold_in(rng, axis), (), 0, length) for axis, length in enumerate(values.shape)]
    main_axis = values.shape.index(max(values.shape))
    neighbour = spot[:main_axis] + [(spot[main_axis] + 1) % values.shape[main_axis]] + spot[main_axis + 1:]
    return values.at[tuple(spot)].set(low).at[tuple(neighbour)].set(top_value)


def shard_levels(own_key, dims, cuts, smallest, high):
    factor_of, own = 1.0, jax.random.fold_in(own_key, 6)
    for position, blocks in cuts:
        steps = jnp.exp(jax.random.uniform(jax.random.fold_in(own, position), (blocks,), jnp.float32, smallest / len(cuts), high / len(cuts)))
        factor_of = factor_of * jnp.repeat(steps, dims[position] // blocks).reshape([-1 if axis == position else 1 for axis in range(len(dims))])
    return factor_of


def noise(own_key, extent, spread, most, cuts=(), kind=jnp.bfloat16):
    factor_of = shard_levels(own_key, extent, cuts, -0.22, 0.18) if cuts else 1.0
    result = jax.random.normal(own_key, extent, jnp.float32) * spread * factor_of
    return jnp.minimum(jnp.maximum(result, -most), most).astype(kind)


def setup_inputs(seed: int = 0) -> dict:
    key_of = jax.random.split(jax.random.key(seed), 7)
    waves = noise(key_of[0], (NK, NV + NC, NR), 1.0, 6.0, ((0, 16), (2, 32)))
    screen = jnp.clip(jnp.exp(jax.random.uniform(key_of[1], (NK, NG), jnp.float32, math.log(0.1), math.log(2.0))), 0.1, 2.0)
    pair_table = place_ends(jax.random.randint(key_of[2], (NK, NK), 0, NK), jax.random.fold_in(key_of[2], 1), 0, NK - 1).astype(jnp.int32)
    plane_map = draw_plane_map(jax.random.fold_in(key_of[6], 71), 0)
    trial = noise(key_of[4], (NK, NV * NC, M), 1.0, 6.0, ((0, 32), (2, 16)))
    probe = noise(key_of[5], (NK, NV * NC, M), 1.0, 6.0, ((0, 16), (2, 32)))
    return {"waves": waves, "screen": screen, "pair_table": pair_table, "plane_map": plane_map, "trial": trial, "probe": probe}


def reference(waves, screen, pair_table, plane_map, trial, probe):
    total_k = waves.shape[0]
    width = NV * NC
    scale = NR ** -0.5

    def block(pair_index):
        first = pair_index // total_k
        second = pair_index % total_k
        left = lax.dynamic_index_in_dim(waves, first, 0, keepdims=False).astype(jnp.float32)
        right = lax.dynamic_index_in_dim(waves, second, 0, keepdims=False).astype(jnp.float32)
        valence = left[:NV, None, :] * right[None, :NV, :]
        conduction = left[NV:, None, :] * right[None, NV:, :]
        vspec = jnp.fft.fft(valence, axis=-1)[..., plane_map] * scale
        cspec = jnp.fft.fft(conduction, axis=-1)[..., plane_map] * scale
        weight = screen[pair_table[first, second]]
        kernel = jnp.einsum("xyg,uwg->uxwy", jnp.real(cspec) * weight, jnp.real(vspec), precision=lax.Precision.HIGHEST)
        kernel = kernel + jnp.einsum("xyg,uwg->uxwy", jnp.imag(cspec) * weight, jnp.imag(vspec), precision=lax.Precision.HIGHEST)
        return (kernel / NG).reshape(width, width)

    blocks = lax.map(block, jnp.arange(total_k * total_k, dtype=jnp.int32))
    blocks = blocks.reshape(total_k, total_k, width, width)
    applied = jnp.einsum("kjab,jbm->kam", blocks, trial.astype(jnp.float32), precision=lax.Precision.HIGHEST)
    adjoint = jnp.einsum("kjab,kam->jbm", blocks, probe.astype(jnp.float32), precision=lax.Precision.HIGHEST)
    return applied, adjoint
```

```python
import math

import jax
import jax.numpy as jnp
import numpy as np
from jax import lax
from jax.experimental import pallas as pl
from jax.experimental.pallas import tpu as pltpu
from jax.sharding import PartitionSpec as P

NV = 8
NC = 8
OUTER = 32
INNER = 128
BLOCK = 56
SLAB = 40
GROUPS = OUTER // 2 + 1
BF = jnp.bfloat16
F32 = jnp.float32


def split_np(values):
    high = np.asarray(values, np.float32).astype(jnp.bfloat16)
    low = (np.asarray(values, np.float64) - high.astype(np.float64)).astype(jnp.bfloat16)
    return high, low


def constants():
    inner = np.arange(INNER)
    angle = 2.0 * np.pi * ((inner[:, None] * inner[None, :]) % INNER) / INNER
    cos, sin = np.cos(angle), np.sin(angle)
    matrix = np.block([[cos, -sin], [sin, cos]])
    high, low = split_np(matrix)
    group = np.arange(GROUPS)
    twist = 2.0 * np.pi * (group[:, None] * inner[None, :]) / (OUTER * INNER)
    table = np.stack([np.cos(twist), np.sin(twist)], axis=1).reshape(2 * GROUPS, 1, INNER)
    table = np.broadcast_to(table, (2 * GROUPS, 8, INNER)).astype(np.float32)
    rows = np.arange(128)
    halves = np.arange(64)
    place = np.zeros((2, 128, 64), np.float32)
    for half in range(2):
        place[half] = rows[:, None] == (halves // 4 * 8 + half * 4 + halves % 4)[None, :]
    lane = np.arange(8 * 64)
    pick = np.arange(64)
    spread = (pick[:, None] // 8 == lane[None, :] // 64) & (pick[:, None] % 8 == lane[None, :] % 8)
    keep = (rows[:, None] % 8) == (lane[None, :] % 64 // 8)
    return (
        high,
        low,
        np.ascontiguousarray(table),
        place.astype(jnp.bfloat16),
        np.ascontiguousarray(np.swapaxes(place, 1, 2)).astype(jnp.bfloat16),
        spread.astype(jnp.bfloat16),
        keep.astype(np.float32),
    )


def real_fft(x):
    n = len(x)
    if n == 2:
        return [x[0] + x[1], x[0] - x[1]], [None, None]
    even_re, even_im = real_fft(x[0::2])
    odd_re, odd_im = real_fft(x[1::2])
    half = n // 2
    out_re, out_im = [None] * (half + 1), [None] * (half + 1)
    out_re[0] = even_re[0] + odd_re[0]
    out_re[half] = even_re[0] - odd_re[0]
    out_re[half // 2] = even_re[half // 2]
    out_im[half // 2] = -odd_re[half // 2]
    for k in range(1, half // 2):
        c, s = math.cos(2 * math.pi * k / n), math.sin(2 * math.pi * k / n)
        if 8 * k == n:
            turn_re = (odd_re[k] + odd_im[k]) * c
            turn_im = (odd_im[k] - odd_re[k]) * c
        else:
            turn_re = odd_re[k] * c + odd_im[k] * s
            turn_im = odd_im[k] * c - odd_re[k] * s
        out_re[k] = even_re[k] + turn_re
        out_im[k] = even_im[k] + turn_im
        out_re[half - k] = even_re[k] - turn_re
        out_im[half - k] = turn_im - even_im[k]
    return out_re, out_im


def split(x):
    high = x.astype(BF)
    return high, (x - high.astype(F32)).astype(BF)


def dot(a, b):
    return lax.dot_general(a, b, (((1,), (0,)), ((), ())), preferred_element_type=F32)


def dot_t(a, b):
    return lax.dot_general(a, b, (((1,), (1,)), ((), ())), preferred_element_type=F32)


def block_kernel(
    data, trial, weight, high, low, table, place, gather, spread, keep, applied, adjoint, wide, grid, acc
):
    wide[...] = data[:, :48, :].astype(F32)

    def transform(i, carry):
        side = pl.multiple_of(32 + (i // 8) % 2 * 8, 8)
        base = pl.multiple_of(i * 8, 8)
        tiles = [
            jnp.broadcast_to(wide[a, pl.ds(i, 1), :], (8, INNER)) * wide[a, pl.ds(side, 8), :] for a in range(OUTER)
        ]
        re, im = real_fft(tiles)
        for c in range(GROUPS):
            if c == 0:
                new_re, new_im = re[0], jnp.zeros_like(re[0])
            elif c == GROUPS - 1:
                new_re, new_im = re[c] * table[2 * c], -(re[c] * table[2 * c + 1])
            else:
                cos, sin = table[2 * c], table[2 * c + 1]
                new_re = re[c] * cos + im[c] * sin
                new_im = im[c] * cos - re[c] * sin
            grid[c, pl.ds(base, 8), :INNER] = new_re
            grid[c, pl.ds(base, 8), INNER:] = new_im
        return carry

    lax.fori_loop(0, 32, transform, 0)
    acc[...] = jnp.zeros_like(acc)

    def contract(c, carry):
        x_high, x_low = split(grid[c])
        s = dot(x_high, high[...]) + dot(x_low, high[...]) + dot(x_high, low[...])
        for q in range(2):
            val = s[q * 128 : q * 128 + 64]
            con = s[q * 128 + 64 : q * 128 + 128]
            w = weight[q, pl.ds(c, 1), :]
            con = con * jnp.concatenate([w, w], axis=1)
            val = jnp.concatenate(split(val), axis=0)
            con = jnp.concatenate(split(con), axis=0)
            acc[q] += dot_t(val, con)
        return carry

    lax.fori_loop(0, GROUPS, contract, 0)

    pair = []
    for q in range(2):
        total = acc[q]
        pair.append(total[:64, :64] + total[:64, 64:] + total[64:, :64] + total[64:, 64:])
    both = jnp.concatenate(pair, axis=0)
    both_high, both_low = split(both)
    moved = (dot(both_high, spread[...]) + dot(both_low, spread[...])) * keep[...]
    moved = moved.reshape(16, 8, 512).sum(axis=1)
    parts = [moved[q * 8 : q * 8 + 8, x * 64 : x * 64 + 64] for q in range(2) for x in range(8)]
    kernel_high, kernel_low = split(jnp.concatenate(parts, axis=0))

    packed = trial[...].astype(BF)
    columns = (dot(place[0], packed[:, :64]) + dot(place[1], packed[:, 64:])).astype(BF)
    applied[...] = dot_t(columns, kernel_high) + dot_t(columns, kernel_low)

    probe = data[:, 48:52, :].reshape(128, 128)
    sides = []
    for half in range(2):
        chosen = dot(gather[half], probe).astype(BF)
        sides.append(dot(chosen, kernel_high) + dot(chosen, kernel_low))
    adjoint[...] = jnp.concatenate(sides, axis=1)


def make_weight(screen, pair_table, plane_map, planes, points):
    chosen = jnp.take(screen, pair_table.reshape(-1), axis=0) * (1.0 / (planes * points))
    group = jnp.arange(GROUPS, dtype=jnp.int32)[:, None]
    other = points - plane_map
    direct = (plane_map % OUTER)[None, :] == group
    mirror = ((other % OUTER)[None, :] == group) & (group > 0) & (group < GROUPS - 1)
    mask = jnp.concatenate([direct, mirror], axis=1).astype(F32)
    left = mask[None] * jnp.concatenate([chosen, chosen], axis=1)[:, None, :]
    spot = jnp.concatenate([plane_map // OUTER, other // OUTER])
    right = (spot[None, :] == jnp.arange(INNER, dtype=jnp.int32)[:, None]).astype(F32)
    return jnp.einsum("qcg,hg->qch", left, right, precision=lax.Precision.HIGHEST)


def local_blocks(data, trial, weight, call=pl.pallas_call):
    vmem = pl.BlockSpec(memory_space=pltpu.VMEM)
    return call(
        block_kernel,
        out_shape=(
            jax.ShapeDtypeStruct((128, 128), F32),
            jax.ShapeDtypeStruct((64, 128), F32),
        ),
        in_specs=[vmem] * 10,
        out_specs=(vmem, vmem),
        scratch_shapes=[
            pltpu.VMEM((OUTER, 48, INNER), F32),
            pltpu.VMEM((GROUPS, 256, 2 * INNER), F32),
            pltpu.VMEM((2, 128, 128), F32),
        ],
        compiler_params=pltpu.CompilerParams(vmem_limit_bytes=32 << 20),
        name="pair_blocks",
    )(data, trial, weight, *constants())


def shards(waves, screen, pair_table, plane_map, trial, probe):
    n_rows = lax.axis_size("ka")
    n_cols = lax.axis_size("kp")
    own = waves.reshape(32, INNER)
    trial_rows = trial.reshape(64, 2, 4).transpose(2, 1, 0).reshape(4, 128)
    probe_rows = probe.reshape(2, 8, 8, 4).transpose(3, 0, 2, 1).reshape(4, 128)
    blank = jnp.zeros((4, 128), BF)

    out = jnp.concatenate([own, trial_rows, blank], axis=0)
    out = jnp.broadcast_to(out[None], (n_rows, SLAB, 128))
    slab = lax.all_to_all(out, "ka", 0, 0, tiled=True)
    trial_full = slab[:, 32:36, :].reshape(64, 128)
    partner = slab[:, :32, :].reshape(n_cols, 16, 128)

    shared = jnp.concatenate([own, probe_rows, blank], axis=0)
    shared = jnp.broadcast_to(shared[None], (n_cols, 40, 128))
    out = jnp.concatenate([shared[:, :32], partner, shared[:, 32:]], axis=1)
    data = lax.all_to_all(out, "kp", 0, 0, tiled=True)

    weight = make_weight(screen, pair_table, plane_map, plane_map.shape[0], OUTER * INNER)
    applied, adjoint = local_blocks(data, trial_full, weight)

    applied = lax.all_to_all(applied.reshape(n_cols, 4, 128), "kp", 0, 0, tiled=True).sum(axis=0)
    adjoint = lax.all_to_all(adjoint.reshape(n_rows, 4, 128), "ka", 0, 0, tiled=True).sum(axis=0)
    applied = applied.reshape(4, 2, 8, 8).transpose(1, 3, 2, 0).reshape(2, 64, 4)
    adjoint = adjoint.reshape(4, 2, 64).transpose(2, 1, 0).reshape(1, 64, 8)
    return applied, adjoint


def solution(mesh):
    placed = (
        P("ka", None, "kp"),
        P(),
        P("ka", "kp"),
        P(),
        P("kp", None, "ka"),
        P("ka", None, "kp"),
    )
    return jax.shard_map(
        shards,
        mesh=mesh,
        in_specs=placed,
        out_specs=(P("ka", None, "kp"), P("kp", None, "ka")),
        check_vma=False,
    )
```

```python
import math

import jax
import jax.numpy as jnp
import numpy as np
from jax import lax
from jax.experimental import pallas as pl
from jax.experimental.pallas import tpu as pltpu
from jax.sharding import PartitionSpec as P

OUTER = 32
INNER = 128
BLOCK = 56
SLAB = 40
GROUPS = OUTER // 2 + 1
UNROLL = 4
BF = jnp.bfloat16
F32 = jnp.float32


def split_np(values):
    high = np.asarray(values, np.float32).astype(jnp.bfloat16)
    low = (np.asarray(values, np.float64) - high.astype(np.float64)).astype(jnp.bfloat16)
    return high, low


def constants():
    inner = np.arange(INNER)
    angle = 2.0 * np.pi * ((inner[:, None] * inner[None, :]) % INNER) / INNER
    cos, sin = np.cos(angle), np.sin(angle)
    high, low = split_np(np.block([[cos, -sin], [sin, cos]]))
    group = np.arange(GROUPS)
    twist = 2.0 * np.pi * (group[:, None] * inner[None, :]) / (OUTER * INNER)
    table = np.stack([np.cos(twist), np.sin(twist)], axis=1).reshape(2 * GROUPS, 1, INNER)
    table = np.broadcast_to(table, (2 * GROUPS, 8, INNER)).astype(np.float32)
    return np.concatenate([high, high, low], axis=0), np.ascontiguousarray(table)


def real_fft(x):
    n = len(x)
    if n == 2:
        return [x[0] + x[1], x[0] - x[1]], [None, None]
    even_re, even_im = real_fft(x[0::2])
    odd_re, odd_im = real_fft(x[1::2])
    half = n // 2
    out_re, out_im = [None] * (half + 1), [None] * (half + 1)
    out_re[0] = even_re[0] + odd_re[0]
    out_re[half] = even_re[0] - odd_re[0]
    out_re[half // 2] = even_re[half // 2]
    out_im[half // 2] = -odd_re[half // 2]
    for k in range(1, half // 2):
        c, s = math.cos(2 * math.pi * k / n), math.sin(2 * math.pi * k / n)
        if 8 * k == n:
            turn_re = (odd_re[k] + odd_im[k]) * c
            turn_im = (odd_im[k] - odd_re[k]) * c
        else:
            turn_re = odd_re[k] * c + odd_im[k] * s
            turn_im = odd_im[k] * c - odd_re[k] * s
        out_re[k] = even_re[k] + turn_re
        out_im[k] = even_im[k] + turn_im
        out_re[half - k] = even_re[k] - turn_re
        out_im[half - k] = turn_im - even_im[k]
    return out_re, out_im


def split(x):
    high = x.astype(BF)
    return high, (x - high.astype(F32)).astype(BF)


def dot(a, b):
    return lax.dot_general(a, b, (((1,), (0,)), ((), ())), preferred_element_type=F32)


def dot_t(a, b):
    return lax.dot_general(a, b, (((1,), (1,)), ((), ())), preferred_element_type=F32)


def first_kernel(own, trial, out):
    rows = jnp.zeros((8, 128 - trial.shape[1]), BF)
    last = jnp.concatenate([trial[...], rows], axis=1)
    for i in range(out.shape[0]):
        out[i, :32, :] = own[...]
        out[i, 32:, :] = last


def second_kernel(own, probe, slab, out):
    for i in range(out.shape[0]):
        out[i, :32, :] = own[...]
        out[i, 32:48, :] = slab[i // 2, i % 2 * 16 : i % 2 * 16 + 16, :]
        out[i, 48:, :] = probe[...]


def last_kernel(parts, out):
    total = parts[...].sum(axis=0)
    out[:4, :] = total[:, :64]
    out[4:, :] = total[:, 64:]


def block_kernel(data, slab, weight, matrix, table, applied, adjoint, wide, grid, val, con, acc):
    wide[...] = data[:, :48, :].astype(F32)

    def transform(i):
        q, t, x = i // 16, i // 8 % 2, i % 8
        single = t * (q * 16 + 8) + (1 - t) * 32 + x
        side = pl.multiple_of(t * 40 + (1 - t) * q * 16, 8)
        base = pl.multiple_of(i * 8, 8)
        tiles = [
            jnp.broadcast_to(wide[a, pl.ds(single, 1), :], (8, INNER)) * wide[a, pl.ds(side, 8), :]
            for a in range(OUTER)
        ]
        re, im = real_fft(tiles)
        for c in range(GROUPS):
            if c == 0:
                new_re, new_im = re[0], jnp.zeros_like(re[0])
            elif c == GROUPS - 1:
                new_re, new_im = re[c] * table[2 * c], -(re[c] * table[2 * c + 1])
            else:
                cos, sin = table[2 * c], table[2 * c + 1]
                new_re = re[c] * cos + im[c] * sin
                new_im = im[c] * cos - re[c] * sin
            grid[c, pl.ds(base, 8), :INNER] = new_re
            grid[c, pl.ds(base, 8), INNER:] = new_im

    def transform_some(i, carry):
        for part in range(UNROLL):
            transform(i * UNROLL + part)
        return carry

    lax.fori_loop(0, 32 // UNROLL, transform_some, 0)
    acc[...] = jnp.zeros_like(acc)

    def spectra(c, count, slot):
        x = grid[pl.ds(c, count)].reshape(count * 256, 256)
        x_high, x_low = split(x)
        s = dot(jnp.concatenate([x_high, x_low, x_high], axis=1), matrix[...])
        for part in range(count):
            for q in range(2):
                w = weight[q, pl.ds(c + part, 1), :]
                w = jnp.concatenate([w, w], axis=1)
                row = part * 256 + q * 128
                lanes = slice(part * 256, part * 256 + 256)
                val[slot, q, :, lanes] = jnp.concatenate(split(s[row : row + 64]), axis=0)
                con[slot, q, :, lanes] = jnp.concatenate(split(s[row + 64 : row + 128] * w), axis=0)

    def contract(slot):
        for q in range(2):
            acc[q] += dot_t(val[slot, q], con[slot, q])

    def four_groups(t, carry):
        spectra(4 * t + 1, 2, 1)
        contract(0)
        spectra(4 * t + 3, 2, 0)
        contract(1)
        return carry

    val[0, :, :, 256:] = jnp.zeros((2, 128, 256), BF)
    con[0, :, :, 256:] = jnp.zeros((2, 128, 256), BF)
    spectra(0, 1, 0)
    lax.fori_loop(0, GROUPS // 4, four_groups, 0)
    contract(0)

    lane = lax.broadcasted_iota(jnp.int32, (64, 128), 1)
    twice = []
    for q in range(2):
        part = acc[q, :64, :] + acc[q, 64:, :]
        twice.append(part + pltpu.roll(part, 64, 1))
    both = jnp.where(lane < 64, twice[0], twice[1])
    spot = lane[:8] // 8 % 8
    rows = []
    for x in range(8):
        row = jnp.zeros((8, 128), F32)
        for w in range(8):
            block = both[w * 8 : w * 8 + 8]
            shift = (w - x) * 8 % 128
            if shift:
                block = pltpu.roll(block, shift, 1)
            row = jnp.where(spot == w, block, row)
        rows.append(row)
    moved = jnp.concatenate(rows, axis=0)
    moved = jnp.concatenate([moved, pltpu.roll(moved, 64, 1)], axis=0)
    high, low = split(moved)

    columns = slab[:, 32:40, :].astype(F32).reshape(128, 128).astype(BF)
    applied[...] = dot_t(columns, high) + dot_t(columns, low)
    probe = data[:, 48:52, :].reshape(128, 128)
    full = dot(probe, high) + dot(probe, low)
    turned = pltpu.roll(pltpu.roll(full, 64, 1), 124, 0)
    wide_lane = lax.broadcasted_iota(jnp.int32, (128, 128), 1)
    full = jnp.where(wide_lane < 64, full, turned).reshape(16, 8, 128)
    adjoint[...] = full[:, :4, :]


def make_weight(screen, pair_table, plane_map, planes, points):
    chosen = jnp.take(screen, pair_table.reshape(-1), axis=0) * (1.0 / (planes * points))
    group = jnp.arange(GROUPS, dtype=jnp.int32)[:, None]
    other = points - plane_map
    direct = (plane_map % OUTER)[None, :] == group
    mirror = ((other % OUTER)[None, :] == group) & (group > 0) & (group < GROUPS - 1)
    mask = jnp.concatenate([direct, mirror], axis=1).astype(F32)
    left = mask[None] * jnp.concatenate([chosen, chosen], axis=1)[:, None, :]
    spot = jnp.concatenate([plane_map // OUTER, other // OUTER])
    right = (spot[None, :] == jnp.arange(INNER, dtype=jnp.int32)[:, None]).astype(F32)
    return jnp.einsum("qcg,hg->qch", left, right, precision=lax.Precision.HIGHEST)


VMEM = pl.BlockSpec(memory_space=pltpu.VMEM)


def call_kernel(body, name, *inputs, outs, scratch=(), limit=16, call=pl.pallas_call):
    return call(
        body,
        out_shape=outs,
        in_specs=[VMEM] * len(inputs),
        out_specs=jax.tree.map(lambda _: VMEM, outs),
        scratch_shapes=scratch,
        compiler_params=pltpu.CompilerParams(vmem_limit_bytes=limit << 20),
        name=name,
    )(*inputs)


def local_blocks(data, slab, weight, call=pl.pallas_call):
    return call_kernel(
        block_kernel,
        "pair_blocks",
        data,
        slab,
        weight,
        *constants(),
        outs=(
            jax.ShapeDtypeStruct((128, 128), F32),
            jax.ShapeDtypeStruct((16, 4, 128), F32),
        ),
        scratch=[
            pltpu.VMEM((OUTER, 48, INNER), F32),
            pltpu.VMEM((GROUPS, 256, 2 * INNER), F32),
            pltpu.VMEM((2, 2, 128, 512), BF),
            pltpu.VMEM((2, 2, 128, 512), BF),
            pltpu.VMEM((2, 128, 128), F32),
        ],
        limit=32,
        call=call,
    )


def shards(waves, screen, pair_table, plane_map, trial, probe):
    n_rows = lax.axis_size("ka")
    n_cols = lax.axis_size("kp")
    own = waves.reshape(32, INNER)
    probe_rows = probe.reshape(2, 8, 8, 4).transpose(3, 0, 2, 1).reshape(4, 128)
    probe_rows = jnp.concatenate([probe_rows, jnp.zeros((4, 128), BF)], axis=0)

    out = call_kernel(
        first_kernel,
        "first",
        own,
        trial.reshape(64, 8).T,
        outs=jax.ShapeDtypeStruct((n_rows, SLAB, 128), BF),
    )
    slab = lax.all_to_all(out, "ka", 0, 0, tiled=True)
    out = call_kernel(
        second_kernel,
        "second",
        own,
        probe_rows,
        slab,
        outs=jax.ShapeDtypeStruct((n_cols, BLOCK, 128), BF),
    )
    data = lax.all_to_all(out, "kp", 0, 0, tiled=True)

    weight = make_weight(screen, pair_table, plane_map, plane_map.shape[0], OUTER * INNER)
    applied, adjoint = local_blocks(data, slab, weight)

    applied = lax.all_to_all(applied.reshape(n_cols, 4, 128), "kp", 0, 0, tiled=True)
    adjoint = lax.all_to_all(adjoint, "ka", 0, 0, tiled=True)
    applied = applied.sum(axis=0)
    applied = applied.reshape(4, 2, 8, 8).transpose(1, 3, 2, 0).reshape(2, 64, 4)
    adjoint = call_kernel(
        last_kernel, "last", adjoint, outs=jax.ShapeDtypeStruct((8, 64), F32)
    )
    return applied, adjoint.T.reshape(1, 64, 8)


def solution(mesh):
    placed = (
        P("ka", None, "kp"),
        P(),
        P("ka", "kp"),
        P(),
        P("kp", None, "ka"),
        P("ka", None, "kp"),
    )
    return jax.shard_map(
        shards,
        mesh=mesh,
        in_specs=placed,
        out_specs=(P("ka", None, "kp"), P("kp", None, "ka")),
        check_vma=False,
    )
```

```python
import math

import jax
import jax.numpy as jnp
import numpy as np
from jax import lax
from jax.experimental import pallas as pl
from jax.experimental.pallas import tpu as pltpu
from jax.sharding import PartitionSpec as P

NV = 8
NC = 8
OUTER = 32
INNER = 128
BLOCK = 56
SLAB = 48
GROUPS = OUTER // 2 + 1
UNROLL = 4
BF = jnp.bfloat16
F32 = jnp.float32


def split_np(values):
    high = np.asarray(values, np.float32).astype(jnp.bfloat16)
    low = (np.asarray(values, np.float64) - high.astype(np.float64)).astype(jnp.bfloat16)
    return high, low


def constants():
    inner = np.arange(INNER)
    angle = 2.0 * np.pi * ((inner[:, None] * inner[None, :]) % INNER) / INNER
    cos, sin = np.cos(angle), np.sin(angle)
    high, low = split_np(np.block([[cos, -sin], [sin, cos]]))
    group = np.arange(GROUPS)
    twist = 2.0 * np.pi * (group[:, None] * inner[None, :]) / (OUTER * INNER)
    table = np.stack([np.cos(twist), np.sin(twist)], axis=1).reshape(2 * GROUPS, 1, INNER)
    table = np.broadcast_to(table, (2 * GROUPS, 8, INNER)).astype(np.float32)
    order = np.zeros((2, 128, 128), np.float32)
    for spot in range(64):
        for side in range(2):
            order[side, side * 64 + spot, spot % 8 * 8 + spot // 8] = 1.0
    return (
        np.concatenate([high, high, low], axis=0),
        np.ascontiguousarray(table),
        order.astype(jnp.bfloat16),
    )


def real_fft(x):
    n = len(x)
    if n == 2:
        return [x[0] + x[1], x[0] - x[1]], [None, None]
    even_re, even_im = real_fft(x[0::2])
    odd_re, odd_im = real_fft(x[1::2])
    half = n // 2
    out_re, out_im = [None] * (half + 1), [None] * (half + 1)
    out_re[0] = even_re[0] + odd_re[0]
    out_re[half] = even_re[0] - odd_re[0]
    out_re[half // 2] = even_re[half // 2]
    out_im[half // 2] = -odd_re[half // 2]
    for k in range(1, half // 2):
        c, s = math.cos(2 * math.pi * k / n), math.sin(2 * math.pi * k / n)
        if 8 * k == n:
            turn_re = (odd_re[k] + odd_im[k]) * c
            turn_im = (odd_im[k] - odd_re[k]) * c
        else:
            turn_re = odd_re[k] * c + odd_im[k] * s
            turn_im = odd_im[k] * c - odd_re[k] * s
        out_re[k] = even_re[k] + turn_re
        out_im[k] = even_im[k] + turn_im
        out_re[half - k] = even_re[k] - turn_re
        out_im[half - k] = turn_im - even_im[k]
    return out_re, out_im


def split(x):
    high = x.astype(BF)
    return high, (x - high.astype(F32)).astype(BF)


def dot(a, b):
    return lax.dot_general(a, b, (((1,), (0,)), ((), ())), preferred_element_type=F32)


def dot_t(a, b):
    return lax.dot_general(a, b, (((1,), (1,)), ((), ())), preferred_element_type=F32)


def first_kernel(pair, own, trial, probe, out, pair_here, own_here, trial_here, probe_here, sems):
    copies = [
        pltpu.make_async_copy(source, target, sems.at[i])
        for i, (source, target) in enumerate(
            ((pair, pair_here), (own, own_here), (trial, trial_here), (probe, probe_here))
        )
    ]
    for copy in copies:
        copy.start()
    for copy in copies:
        copy.wait()
    side = jnp.concatenate([trial_here[...], probe_here[...]], axis=1)
    spot = lax.broadcasted_iota(jnp.int32, (8, 128), 0)
    index = jnp.where(spot == 0, pair_here[0], pair_here[1]).astype(F32).astype(BF)
    for i in range(out.shape[0]):
        out[i, :32, :] = own_here[...]
        out[i, 32:40, :] = side
        out[i, 40:, :] = index


def second_kernel(own, slab, out):
    for i in range(out.shape[0]):
        half = i % 2
        out[i, :32, :] = own[...]
        out[i, 32:48, :] = slab[i // 2, half * 16 : half * 16 + 16, :]
        rest = slab[i // 2, 32:48, :].astype(F32)
        index = jnp.broadcast_to(rest[8 + half : 9 + half], (4, 128))
        rest = jnp.concatenate([rest[half * 4 : half * 4 + 4], index], axis=0)
        out[i, 48:, :] = rest.astype(BF)


def last_kernel(parts, applied, adjoint):
    total = parts[...].sum(axis=0)
    applied[0] = total[:4, :64]
    applied[1] = total[:4, 64:]
    adjoint[:4, :] = total[4:, :64]
    adjoint[4:, :] = total[4:, 64:]


def blocks_moved(both):
    spot = lax.broadcasted_iota(jnp.int32, (8, 128), 1) // 8 % 8
    rows = []
    for new in range(8):
        row = jnp.zeros((8, 128), F32)
        for old in range(8):
            block = both[old * 8 : old * 8 + 8]
            shift = (old - new) * 8 % 128
            if shift:
                block = pltpu.roll(block, shift, 1)
            row = jnp.where(spot == old, block, row)
        rows.append(row)
    moved = jnp.concatenate(rows, axis=0)
    return jnp.concatenate([moved, pltpu.roll(moved, 64, 1)], axis=0)


def block_kernel(
    pair, place, data, slab, screens, matrix, table, order, out, wide, grid, val, con, acc, weight
):
    wide[...] = data[:, :48, :].astype(F32)
    for q in range(2):
        weight[q] = screens[pair[q]]
        other = data[pl.ds(2 * place[0] + q, 1), 52:56, :].astype(F32)
        weight[2 + q] = screens[jnp.max(other).astype(jnp.int32)]

    def transform(i):
        q, t, s = i // 16, i // 8 % 2, i % 8
        single = (1 - t) * (q * 16) + t * 40 + s
        side = pl.multiple_of((1 - t) * 32 + t * (q * 16 + 8), 8)
        base = pl.multiple_of(i * 8, 8)
        tiles = [
            jnp.broadcast_to(wide[a, pl.ds(single, 1), :], (8, INNER)) * wide[a, pl.ds(side, 8), :]
            for a in range(OUTER)
        ]
        re, im = real_fft(tiles)
        for c in range(GROUPS):
            if c == 0:
                new_re, new_im = re[0], jnp.zeros_like(re[0])
            elif c == GROUPS - 1:
                new_re, new_im = re[c] * table[2 * c], -(re[c] * table[2 * c + 1])
            else:
                cos, sin = table[2 * c], table[2 * c + 1]
                new_re = re[c] * cos + im[c] * sin
                new_im = im[c] * cos - re[c] * sin
            grid[c, pl.ds(base, 8), :INNER] = new_re
            grid[c, pl.ds(base, 8), INNER:] = new_im

    def transform_some(i, carry):
        for part in range(UNROLL):
            transform(i * UNROLL + part)
        return carry

    lax.fori_loop(0, 32 // UNROLL, transform_some, 0)
    acc[...] = jnp.zeros_like(acc)

    def spectra(c, count, slot):
        x = grid[pl.ds(c, count)].reshape(count * 256, 256)
        x_high, x_low = split(x)
        s = dot(jnp.concatenate([x_high, x_low, x_high], axis=1), matrix[...])
        for part in range(count):
            lanes = slice(part * 256, part * 256 + 256)
            for q in range(2):
                row = part * 256 + q * 128
                val[slot, q, :, lanes] = jnp.concatenate(split(s[row : row + 64]), axis=0)
                for side in range(2):
                    w = weight[2 * side + q, pl.ds(c + part, 1), :]
                    w = jnp.concatenate([w, w], axis=1)
                    rows = slice(side * 128, side * 128 + 128)
                    con[slot, q, rows, lanes] = jnp.concatenate(
                        split(s[row + 64 : row + 128] * w), axis=0
                    )

    def contract(slot):
        for q in range(2):
            acc[q] += dot_t(con[slot, q], val[slot, q])

    def four_groups(t, carry):
        spectra(4 * t + 1, 2, 1)
        contract(0)
        spectra(4 * t + 3, 2, 0)
        contract(1)
        return carry

    val[0, :, :, 256:] = jnp.zeros((2, 128, 256), BF)
    con[0, :, :, 256:] = jnp.zeros((2, 256, 256), BF)
    spectra(0, 1, 0)
    lax.fori_loop(0, GROUPS // 4, four_groups, 0)
    contract(0)

    inputs = (slab[:, 32:40, :].astype(F32).reshape(128, 128), data[:, 48:52, :].reshape(128, 128))
    lane = lax.broadcasted_iota(jnp.int32, (64, 128), 1)
    results = []
    for side in range(2):
        twice = []
        for q in range(2):
            part = acc[q, side * 128 : side * 128 + 64, :]
            part = part + acc[q, side * 128 + 64 : side * 128 + 128, :]
            twice.append(part + pltpu.roll(part, 64, 1))
        high, low = split(blocks_moved(jnp.where(lane < 64, twice[0], twice[1])))
        columns = dot(inputs[side].astype(BF), order[side]).astype(BF)
        results.append(dot_t(columns, high) + dot_t(columns, low))

    first, full = results
    lane = lax.broadcasted_iota(jnp.int32, (128, 128), 1)
    spot = lax.broadcasted_iota(jnp.int32, (128, 128), 0) % 8
    down = pltpu.roll(full, 4, 0)
    even = jnp.where(lane < 64, down, pltpu.roll(full, 64, 1))
    odd = jnp.where(lane < 64, pltpu.roll(down, 64, 1), full)
    even = jnp.where(spot < 4, first, even)
    odd = jnp.where(spot < 4, pltpu.roll(first, 124, 0), odd)
    out[:, 0] = even.reshape(16, 8, 128)
    out[:, 1] = odd.reshape(16, 8, 128)


def make_weight(screen, plane_map, planes, points):
    chosen = screen * (1.0 / (planes * points))
    group = jnp.arange(GROUPS, dtype=jnp.int32)[:, None]
    other = points - plane_map
    direct = (plane_map % OUTER)[None, :] == group
    mirror = ((other % OUTER)[None, :] == group) & (group > 0) & (group < GROUPS - 1)
    mask = jnp.concatenate([direct, mirror], axis=1).astype(F32)
    left = mask[None] * jnp.concatenate([chosen, chosen], axis=1)[:, None, :]
    spot = jnp.concatenate([plane_map // OUTER, other // OUTER])
    right = (spot[None, :] == jnp.arange(INNER, dtype=jnp.int32)[:, None]).astype(F32)
    return jnp.einsum("qcg,hg->qch", left, right, precision=lax.Precision.HIGHEST)


VMEM = pl.BlockSpec(memory_space=pltpu.VMEM)
SMEM = pl.BlockSpec(memory_space=pltpu.SMEM)


def call_kernel(
    body, name, *inputs, outs, scalars=0, space=VMEM, scratch=(), limit=16, call=pl.pallas_call
):
    return call(
        body,
        out_shape=outs,
        in_specs=[SMEM] * scalars + [space] * (len(inputs) - scalars),
        out_specs=jax.tree.map(lambda _: VMEM, outs),
        scratch_shapes=scratch,
        compiler_params=pltpu.CompilerParams(vmem_limit_bytes=limit << 20),
        name=name,
    )(*inputs)


def local_blocks(pair, place, data, slab, screens, call=pl.pallas_call):
    return call_kernel(
        block_kernel,
        "pair_blocks",
        pair,
        place,
        data,
        slab,
        screens,
        *constants(),
        scalars=2,
        outs=jax.ShapeDtypeStruct((16, 2, 8, 128), F32),
        scratch=[
            pltpu.VMEM((OUTER, 48, INNER), F32),
            pltpu.VMEM((GROUPS, 256, 2 * INNER), F32),
            pltpu.VMEM((2, 2, 128, 512), BF),
            pltpu.VMEM((2, 2, 256, 512), BF),
            pltpu.VMEM((2, 256, 128), F32),
            pltpu.VMEM((4, GROUPS, INNER), F32),
        ],
        limit=32,
        call=call,
    )


def shards(waves, screen, pair_table, plane_map, trial, probe):
    n_rows = lax.axis_size("ka")
    n_cols = lax.axis_size("kp")
    own = waves.reshape(32, INNER)
    pair = pair_table.reshape(2)
    place = lax.axis_index("ka").astype(jnp.int32).reshape(1)

    stay = (pair, own, trial.reshape(64, 8).T, probe.transpose(0, 2, 1).reshape(8, 64))
    stay = [pltpu.with_memory_space_constraint(x, pltpu.HBM) for x in stay]
    out = call_kernel(
        first_kernel,
        "first",
        *stay,
        space=pl.BlockSpec(memory_space=pltpu.HBM),
        outs=jax.ShapeDtypeStruct((n_rows, SLAB, 128), BF),
        scratch=[
            pltpu.SMEM((2,), jnp.int32),
            pltpu.VMEM((32, 128), BF),
            pltpu.VMEM((8, 64), BF),
            pltpu.VMEM((8, 64), BF),
            pltpu.SemaphoreType.DMA((4,)),
        ],
    )
    slab = lax.all_to_all(out, "ka", 0, 0, tiled=True)
    out = call_kernel(
        second_kernel, "second", own, slab, outs=jax.ShapeDtypeStruct((n_cols, BLOCK, 128), BF)
    )
    data = lax.all_to_all(out, "kp", 0, 0, tiled=True)

    screens = make_weight(screen, plane_map, plane_map.shape[0], OUTER * INNER)
    out = local_blocks(pair, place, data, slab, screens)

    parts = lax.all_to_all(out.reshape(n_cols, 8, 128), "kp", 0, 0, tiled=True)
    applied, adjoint = call_kernel(
        last_kernel,
        "last",
        parts,
        outs=(jax.ShapeDtypeStruct((2, 4, 64), F32), jax.ShapeDtypeStruct((8, 64), F32)),
    )
    swap = [
        (a * n_cols + 2 * b + c, b * n_cols + 2 * a + c)
        for a in range(n_rows)
        for b in range(n_rows)
        for c in range(2)
    ]
    adjoint = lax.ppermute(adjoint, ("ka", "kp"), swap)
    return applied.transpose(0, 2, 1), adjoint.T.reshape(1, 64, 8)


def solution(mesh):
    placed = (
        P("ka", None, "kp"),
        P(),
        P("ka", "kp"),
        P(),
        P("kp", None, "ka"),
        P("ka", None, "kp"),
    )
    return jax.shard_map(
        shards,
        mesh=mesh,
        in_specs=placed,
        out_specs=(P("ka", None, "kp"), P("kp", None, "ka")),
        check_vma=False,
    )
```

```python
import math

import jax
import jax.numpy as jnp
import numpy as np
from jax import lax
from jax.experimental import pallas as pl
from jax.experimental.pallas import tpu as pltpu
from jax.sharding import PartitionSpec as P

NV = 8
NC = 8
OUTER = 32
INNER = 128
BLOCK = 56
SLAB = 48
GROUPS = OUTER // 2 + 1
UNROLL = 4
TURNS = (1, 0, 0, 3)
BF = jnp.bfloat16
F32 = jnp.float32


def split_np(values):
    high = np.asarray(values, np.float32).astype(jnp.bfloat16)
    low = (np.asarray(values, np.float64) - high.astype(np.float64)).astype(jnp.bfloat16)
    return high, low


def constants():
    inner = np.arange(INNER)
    angle = 2.0 * np.pi * ((inner[:, None] * inner[None, :]) % INNER) / INNER
    cos, sin = np.cos(angle), np.sin(angle)
    high, low = split_np(np.block([[cos, -sin], [sin, cos]]))
    group = np.arange(GROUPS)
    twist = 2.0 * np.pi * (group[:, None] * inner[None, :]) / (OUTER * INNER)
    table = np.stack([np.cos(twist), np.sin(twist)], axis=1).reshape(2 * GROUPS, 1, INNER)
    table = np.broadcast_to(table, (2 * GROUPS, 8, INNER)).astype(np.float32)
    order = np.zeros((2, 128, 128), np.float32)
    for spot in range(64):
        for side in range(2):
            order[side, side * 64 + spot, spot % 8 * 8 + spot // 8] = 1.0
    return (
        np.concatenate([high, high, low], axis=0),
        np.ascontiguousarray(table),
        order.astype(jnp.bfloat16),
    )


def real_fft(x):
    n = len(x)
    if n == 2:
        return [x[0] + x[1], x[0] - x[1]], [None, None]
    even_re, even_im = real_fft(x[0::2])
    odd_re, odd_im = real_fft(x[1::2])
    half = n // 2
    out_re, out_im = [None] * (half + 1), [None] * (half + 1)
    out_re[0] = even_re[0] + odd_re[0]
    out_re[half] = even_re[0] - odd_re[0]
    out_re[half // 2] = even_re[half // 2]
    out_im[half // 2] = -odd_re[half // 2]
    for k in range(1, half // 2):
        c, s = math.cos(2 * math.pi * k / n), math.sin(2 * math.pi * k / n)
        if 8 * k == n:
            turn_re = (odd_re[k] + odd_im[k]) * c
            turn_im = (odd_im[k] - odd_re[k]) * c
        else:
            turn_re = odd_re[k] * c + odd_im[k] * s
            turn_im = odd_im[k] * c - odd_re[k] * s
        out_re[k] = even_re[k] + turn_re
        out_im[k] = even_im[k] + turn_im
        out_re[half - k] = even_re[k] - turn_re
        out_im[half - k] = turn_im - even_im[k]
    return out_re, out_im


def split(x):
    high = x.astype(BF)
    return high, (x - high.astype(F32)).astype(BF)


def dot(a, b):
    return lax.dot_general(a, b, (((1,), (0,)), ((), ())), preferred_element_type=F32)


def dot_t(a, b):
    return lax.dot_general(a, b, (((1,), (1,)), ((), ())), preferred_element_type=F32)


def first_kernel(pair, own, trial, probe, out, pair_here, own_here, trial_here, probe_here, sems):
    copies = [
        pltpu.make_async_copy(source, target, sems.at[i])
        for i, (source, target) in enumerate(
            ((pair, pair_here), (own, own_here), (trial, trial_here), (probe, probe_here))
        )
    ]
    for copy in copies:
        copy.start()
    for copy in copies:
        copy.wait()
    side = jnp.concatenate([trial_here[...], probe_here[...]], axis=1)
    spot = lax.broadcasted_iota(jnp.int32, (8, 128), 0)
    index = jnp.where(spot == 0, pair_here[0], pair_here[1]).astype(F32).astype(BF)
    for i in range(out.shape[0]):
        out[i, :32, :] = own_here[...]
        out[i, 32:40, :] = side
        out[i, 40:, :] = index


def second_kernel(own, slab, out):
    for i in range(out.shape[0]):
        half = i % 2
        out[i, :32, :] = own[...]
        out[i, 32:48, :] = slab[i // 2, half * 16 : half * 16 + 16, :]
        rest = slab[i // 2, 32:48, :].astype(F32)
        index = jnp.broadcast_to(rest[8 + half : 9 + half], (4, 128))
        rest = jnp.concatenate([rest[half * 4 : half * 4 + 4], index], axis=0)
        out[i, 48:, :] = rest.astype(BF)


def last_kernel(parts, applied, adjoint):
    total = parts[...].sum(axis=0)
    applied[0] = total[:4, :64]
    applied[1] = total[:4, 64:]
    adjoint[:4, :] = total[4:, :64]
    adjoint[4:, :] = total[4:, 64:]


def blocks_moved(both):
    spot = lax.broadcasted_iota(jnp.int32, (8, 128), 1) // 8 % 8
    rows = []
    for new in range(8):
        row = jnp.zeros((8, 128), F32)
        for old in range(8):
            block = both[old * 8 : old * 8 + 8]
            shift = (old - new) * 8 % 128
            if shift:
                block = pltpu.roll(block, shift, 1)
            row = jnp.where(spot == old, block, row)
        rows.append(row)
    moved = jnp.concatenate(rows, axis=0)
    return jnp.concatenate([moved, pltpu.roll(moved, 64, 1)], axis=0)


def block_kernel(
    pair, place, data, slab, screens, matrix, table, order, out, wide, grid, val, con, acc, weight
):
    wide[...] = data[:, :48, :].astype(F32)
    for q in range(2):
        weight[q] = screens[pair[q]]
        other = data[pl.ds(2 * place[0] + q, 1), 52:56, :].astype(F32)
        weight[2 + q] = screens[jnp.max(other).astype(jnp.int32)]

    def transform(i):
        q, t, s = i // 16, i // 8 % 2, i % 8
        single = (1 - t) * (q * 16) + t * 40 + s
        side = pl.multiple_of((1 - t) * 32 + t * (q * 16 + 8), 8)
        base = pl.multiple_of(i * 8, 8)
        tiles = [
            jnp.broadcast_to(wide[a, pl.ds(single, 1), :], (8, INNER)) * wide[a, pl.ds(side, 8), :]
            for a in range(OUTER)
        ]
        re, im = real_fft(tiles)
        for c in range(GROUPS):
            if c == 0:
                new_re, new_im = re[0], jnp.zeros_like(re[0])
            elif c == GROUPS - 1:
                new_re, new_im = re[c] * table[2 * c], -(re[c] * table[2 * c + 1])
            else:
                cos, sin = table[2 * c], table[2 * c + 1]
                new_re = re[c] * cos + im[c] * sin
                new_im = im[c] * cos - re[c] * sin
            grid[c, pl.ds(base, 8), :INNER] = new_re
            grid[c, pl.ds(base, 8), INNER:] = new_im

    def transform_some(i, carry):
        for part in range(UNROLL):
            transform(i * UNROLL + part)
        return carry

    lax.fori_loop(0, 32 // UNROLL, transform_some, 0)
    acc[...] = jnp.zeros_like(acc)

    def spectra(c, count, slot):
        x = grid[pl.ds(c, count)].reshape(count * 256, 256)
        x_high, x_low = split(x)
        s = dot(jnp.concatenate([x_high, x_low, x_high], axis=1), matrix[...])
        for part in range(count):
            lanes = slice(part * 256, part * 256 + 256)
            for q in range(2):
                row = part * 256 + q * 128
                val[slot, q, :, lanes] = jnp.concatenate(split(s[row : row + 64]), axis=0)
                for side in range(2):
                    w = weight[2 * side + q, pl.ds(c + part, 1), :]
                    w = jnp.concatenate([w, w], axis=1)
                    rows = slice(side * 128, side * 128 + 128)
                    con[slot, q, rows, lanes] = jnp.concatenate(
                        split(s[row + 64 : row + 128] * w), axis=0
                    )

    def contract(slot):
        for q in range(2):
            acc[q] += dot_t(con[slot, q], val[slot, q])

    def four_groups(t, carry):
        spectra(4 * t + 1, 2, 1)
        contract(0)
        spectra(4 * t + 3, 2, 0)
        contract(1)
        return carry

    val[0, :, :, 256:] = jnp.zeros((2, 128, 256), BF)
    con[0, :, :, 256:] = jnp.zeros((2, 256, 256), BF)
    spectra(0, 1, 0)
    lax.fori_loop(0, GROUPS // 4, four_groups, 0)
    contract(0)

    inputs = (slab[:, 32:40, :].astype(F32).reshape(128, 128), data[:, 48:52, :].reshape(128, 128))
    lane = lax.broadcasted_iota(jnp.int32, (64, 128), 1)
    results = []
    for side in range(2):
        twice = []
        for q in range(2):
            part = acc[q, side * 128 : side * 128 + 64, :]
            part = part + acc[q, side * 128 + 64 : side * 128 + 128, :]
            twice.append(part + pltpu.roll(part, 64, 1))
        high, low = split(blocks_moved(jnp.where(lane < 64, twice[0], twice[1])))
        columns = dot(inputs[side].astype(BF), order[side]).astype(BF)
        results.append(dot_t(columns, high) + dot_t(columns, low))

    first, full = results
    lane = lax.broadcasted_iota(jnp.int32, (128, 128), 1)
    down = pltpu.roll(full, 4, 0)
    even = jnp.where(lane < 64, down, pltpu.roll(full, 64, 1))
    odd = jnp.where(lane < 64, pltpu.roll(down, 64, 1), full)
    first = first.reshape(16, 8, 128)
    for i in range(32):
        out[i // 8, i % 8, :4, :] = first[i // 2, i % 2 * 4 : i % 2 * 4 + 4, :]
    zone = place[0] // 4
    turn = jnp.where(zone == 0, TURNS[0], jnp.where(zone == 3, TURNS[3], 0))
    for i in range(32):
        spot = jnp.bitwise_and(i // 8 + turn, 3)
        value = (even, odd)[i % 2][i // 2 * 8 + 4 : i // 2 * 8 + 8, :]
        out[spot, (i // 2 + 2) % 4 * 2 + i % 2, 4:, :] = value


def make_weight(screen, plane_map, planes, points):
    chosen = screen * (1.0 / (planes * points))
    group = jnp.arange(GROUPS, dtype=jnp.int32)[:, None]
    other = points - plane_map
    direct = (plane_map % OUTER)[None, :] == group
    mirror = ((other % OUTER)[None, :] == group) & (group > 0) & (group < GROUPS - 1)
    mask = jnp.concatenate([direct, mirror], axis=1).astype(F32)
    left = mask[None] * jnp.concatenate([chosen, chosen], axis=1)[:, None, :]
    spot = jnp.concatenate([plane_map // OUTER, other // OUTER])
    right = (spot[None, :] == jnp.arange(INNER, dtype=jnp.int32)[:, None]).astype(F32)
    return jnp.einsum("qcg,hg->qch", left, right, precision=lax.Precision.HIGHEST)


VMEM = pl.BlockSpec(memory_space=pltpu.VMEM)
SMEM = pl.BlockSpec(memory_space=pltpu.SMEM)


def call_kernel(
    body, name, *inputs, outs, scalars=0, space=VMEM, scratch=(), limit=16, call=pl.pallas_call
):
    return call(
        body,
        out_shape=outs,
        in_specs=[SMEM] * scalars + [space] * (len(inputs) - scalars),
        out_specs=jax.tree.map(lambda _: VMEM, outs),
        scratch_shapes=scratch,
        compiler_params=pltpu.CompilerParams(vmem_limit_bytes=limit << 20),
        name=name,
    )(*inputs)


def local_blocks(pair, place, data, slab, screens, call=pl.pallas_call):
    return call_kernel(
        block_kernel,
        "pair_blocks",
        pair,
        place,
        data,
        slab,
        screens,
        *constants(),
        scalars=2,
        outs=jax.ShapeDtypeStruct((4, 8, 8, 128), F32),
        scratch=[
            pltpu.VMEM((OUTER, 48, INNER), F32),
            pltpu.VMEM((GROUPS, 256, 2 * INNER), F32),
            pltpu.VMEM((2, 2, 128, 512), BF),
            pltpu.VMEM((2, 2, 256, 512), BF),
            pltpu.VMEM((2, 256, 128), F32),
            pltpu.VMEM((4, GROUPS, INNER), F32),
        ],
        limit=32,
        call=call,
    )


def shards(waves, screen, pair_table, plane_map, trial, probe):
    n_rows = lax.axis_size("ka")
    n_cols = lax.axis_size("kp")
    own = waves.reshape(32, INNER)
    pair = pair_table.reshape(2)
    place = lax.axis_index("ka").astype(jnp.int32).reshape(1)

    stay = (pair, own, trial.reshape(64, 8).T, probe.transpose(0, 2, 1).reshape(8, 64))
    stay = [pltpu.with_memory_space_constraint(x, pltpu.HBM) for x in stay]
    out = call_kernel(
        first_kernel,
        "first",
        *stay,
        space=pl.BlockSpec(memory_space=pltpu.HBM),
        outs=jax.ShapeDtypeStruct((n_rows, SLAB, 128), BF),
        scratch=[
            pltpu.SMEM((2,), jnp.int32),
            pltpu.VMEM((32, 128), BF),
            pltpu.VMEM((8, 64), BF),
            pltpu.VMEM((8, 64), BF),
            pltpu.SemaphoreType.DMA((4,)),
        ],
    )
    slab = lax.all_to_all(out, "ka", 0, 0, tiled=True)
    out = call_kernel(
        second_kernel, "second", own, slab, outs=jax.ShapeDtypeStruct((n_cols, BLOCK, 128), BF)
    )
    data = lax.all_to_all(out, "kp", 0, 0, tiled=True)

    screens = make_weight(screen, plane_map, plane_map.shape[0], OUTER * INNER)
    out = local_blocks(pair, place, data, slab, screens)

    parts = lax.all_to_all(out.reshape(n_cols, 8, 128), "kp", 0, 0, tiled=True)
    applied, adjoint = call_kernel(
        last_kernel,
        "last",
        parts,
        outs=(jax.ShapeDtypeStruct((2, 4, 64), F32), jax.ShapeDtypeStruct((8, 64), F32)),
    )
    swap = []
    for a in range(n_rows):
        for b in range(n_rows):
            for c in range(2):
                spot = (b // 4 + TURNS[a // 4]) % 4 * 8 + (b + 2) % 4 * 2 + c
                swap.append((a * n_cols + spot, b * n_cols + 2 * a + c))
    adjoint = lax.ppermute(adjoint, ("ka", "kp"), swap)
    return applied.transpose(0, 2, 1), adjoint.T.reshape(1, 64, 8)


def solution(mesh):
    placed = (
        P("ka", None, "kp"),
        P(),
        P("ka", "kp"),
        P(),
        P("kp", None, "ka"),
        P("ka", None, "kp"),
    )
    return jax.shard_map(
        shards,
        mesh=mesh,
        in_specs=placed,
        out_specs=(P("ka", None, "kp"), P("kp", None, "ka")),
        check_vma=False,
    )
```

```python
import math

import jax
import jax.numpy as jnp
import numpy as np
from jax import lax
from jax.experimental import pallas as pl
from jax.experimental.pallas import tpu as pltpu
from jax.sharding import PartitionSpec as P

NV = 8
NC = 8
OUTER = 32
INNER = 128
BLOCK = 56
SLAB = 48
GROUPS = OUTER // 2
UNROLL = 4
TURNS = (1, 0, 0, 3)
BF = jnp.bfloat16
F32 = jnp.float32


def split_np(values):
    high = np.asarray(values, np.float32).astype(jnp.bfloat16)
    low = (np.asarray(values, np.float64) - high.astype(np.float64)).astype(jnp.bfloat16)
    return high, low


def constants():
    points = OUTER * INNER
    inner = np.arange(INNER)

    def angle(frequency):
        return 2.0 * np.pi * ((inner[:, None] * frequency[None, :]) % points) / points

    base = angle(OUTER * inner)
    group = angle(np.arange(GROUPS))
    turns = np.concatenate([np.cos(group), np.sin(group), np.zeros((INNER, 96))], axis=1)
    even = OUTER * np.arange(INNER // 2 + 1)
    middle = GROUPS + OUTER * np.arange(INNER // 2)
    zero = np.zeros((INNER, INNER))
    edge = np.block(
        [
            [np.cos(angle(even)), -np.sin(angle(even[1:-1])), zero],
            [zero, np.cos(angle(middle)), -np.sin(angle(middle))],
        ]
    )
    return (
        np.stack([np.cos(base), np.sin(base)]).astype(np.float32),
        turns.astype(np.float32),
        np.concatenate(split_np(edge), axis=0),
    )


def orders():
    order = np.zeros((2, 128, 128), np.float32)
    for spot in range(64):
        for side in range(2):
            order[side, side * 64 + spot, spot % 8 * 8 + spot // 8] = 1.0
    return order.astype(jnp.bfloat16)


def real_fft(x):
    n = len(x)
    if n == 2:
        return [x[0] + x[1], x[0] - x[1]], [None, None]
    even_re, even_im = real_fft(x[0::2])
    odd_re, odd_im = real_fft(x[1::2])
    half = n // 2
    out_re, out_im = [None] * (half + 1), [None] * (half + 1)
    out_re[0] = even_re[0] + odd_re[0]
    out_re[half] = even_re[0] - odd_re[0]
    out_re[half // 2] = even_re[half // 2]
    out_im[half // 2] = -odd_re[half // 2]
    for k in range(1, half // 2):
        c, s = math.cos(2 * math.pi * k / n), math.sin(2 * math.pi * k / n)
        if 8 * k == n:
            turn_re = (odd_re[k] + odd_im[k]) * c
            turn_im = (odd_im[k] - odd_re[k]) * c
        else:
            turn_re = odd_re[k] * c + odd_im[k] * s
            turn_im = odd_im[k] * c - odd_re[k] * s
        out_re[k] = even_re[k] + turn_re
        out_im[k] = even_im[k] + turn_im
        out_re[half - k] = even_re[k] - turn_re
        out_im[half - k] = turn_im - even_im[k]
    return out_re, out_im


def split(x):
    high = x.astype(BF)
    return high, (x - high.astype(F32)).astype(BF)


def dot(a, b):
    return lax.dot_general(a, b, (((1,), (0,)), ((), ())), preferred_element_type=F32)


def dot_t(a, b):
    return lax.dot_general(a, b, (((1,), (1,)), ((), ())), preferred_element_type=F32)


def first_kernel(pair, own, trial, probe, out, pair_here, own_here, trial_here, probe_here, sems):
    copies = [
        pltpu.make_async_copy(source, target, sems.at[i])
        for i, (source, target) in enumerate(
            ((pair, pair_here), (own, own_here), (trial, trial_here), (probe, probe_here))
        )
    ]
    for copy in copies:
        copy.start()
    for copy in copies:
        copy.wait()
    side = jnp.concatenate([trial_here[...], probe_here[...]], axis=1)
    spot = lax.broadcasted_iota(jnp.int32, (8, 128), 0)
    index = jnp.where(spot == 0, pair_here[0], pair_here[1]).astype(F32).astype(BF)
    for i in range(out.shape[0]):
        out[i, :32, :] = own_here[...]
        out[i, 32:40, :] = side
        out[i, 40:, :] = index


def turns_kernel(base, turns, edge, out):
    out[0] = edge[...]
    for c in range(1, GROUPS):
        cos = jnp.broadcast_to(turns[:, c : c + 1], (INNER, INNER))
        sin = jnp.broadcast_to(turns[:, GROUPS + c : GROUPS + c + 1], (INNER, INNER))
        near = split(base[0] * cos - base[1] * sin)
        far = base[1] * cos + base[0] * sin
        back = split(-far)
        far = split(far)
        for level in range(2):
            low, high = level * 256, level * 256 + 128
            out[c, low:high, :128] = near[level]
            out[c, low:high, 128:] = back[level]
            out[c, high : high + 128, :128] = far[level]
            out[c, high : high + 128, 128:] = near[level]


def second_kernel(place, slab, out):
    own = slab[pl.ds(place[0], 1), :32, :].reshape(32, 128)
    for i in range(out.shape[0]):
        half = i % 2
        out[i, :32, :] = own
        out[i, 32:48, :] = slab[i // 2, half * 16 : half * 16 + 16, :]
        rest = slab[i // 2, 32:48, :].astype(F32)
        index = jnp.broadcast_to(rest[8 + half : 9 + half], (4, 128))
        rest = jnp.concatenate([rest[half * 4 : half * 4 + 4], index], axis=0)
        out[i, 48:, :] = rest.astype(BF)


def last_kernel(block, out):
    out[:4, :] = block[:, :64]
    out[4:, :] = block[:, 64:]


def blocks_moved(both):
    spot = lax.broadcasted_iota(jnp.int32, (8, 128), 1) // 8 % 8
    rows = []
    for new in range(8):
        row = jnp.zeros((8, 128), F32)
        for old in range(8):
            block = both[old * 8 : old * 8 + 8]
            shift = (old - new) * 8 % 128
            if shift:
                block = pltpu.roll(block, shift, 1)
            row = jnp.where(spot == old, block, row)
        rows.append(row)
    moved = jnp.concatenate(rows, axis=0)
    return jnp.concatenate([moved, pltpu.roll(moved, 64, 1)], axis=0)


def block_kernel(
    pair,
    place,
    data,
    slab,
    screens,
    turns,
    order,
    out,
    wide,
    grid,
    val,
    con,
    acc,
    weight,
    columns,
    matrix,
    sems,
):
    pieces = [
        pltpu.make_async_copy(turns.at[low:high], matrix.at[low:high], sems.at[i])
        for i, (low, high) in enumerate(((0, 2), (2, GROUPS)))
    ]
    for piece in pieces:
        piece.start()
    wide[...] = data[:, :48, :].astype(F32)
    for q in range(2):
        weight[q] = screens[pair[q]]
        other = data[pl.ds(2 * place[0] + q, 1), 52:56, :].astype(F32)
        weight[2 + q] = screens[jnp.max(other).astype(jnp.int32)]

    def transform(i):
        q, t, s = i // 16, i // 8 % 2, i % 8
        single = (1 - t) * (q * 16) + t * 40 + s
        side = pl.multiple_of((1 - t) * 32 + t * (q * 16 + 8), 8)
        base = pl.multiple_of(i * 8, 8)
        tiles = [
            jnp.broadcast_to(wide[a, pl.ds(single, 1), :], (8, INNER)) * wide[a, pl.ds(side, 8), :]
            for a in range(OUTER)
        ]
        re, im = real_fft(tiles)
        grid[0, pl.ds(base, 8), :INNER] = re[0]
        grid[0, pl.ds(base, 8), INNER:] = re[GROUPS]
        for c in range(1, GROUPS):
            grid[c, pl.ds(base, 8), :INNER] = re[c]
            grid[c, pl.ds(base, 8), INNER:] = im[c]

    def transform_some(i, carry):
        for part in range(UNROLL):
            transform(i * UNROLL + part)
        return carry

    lax.fori_loop(0, 32 // UNROLL, transform_some, 0)
    acc[...] = jnp.zeros_like(acc)
    inputs = (slab[:, 32:40, :].astype(F32).reshape(128, 128), data[:, 48:52, :].reshape(128, 128))
    for side in range(2):
        columns[side] = dot(inputs[side].astype(BF), order[side]).astype(BF)

    def spectra(c, slot):
        for part in range(2):
            x_high, x_low = split(grid[c + part])
            high = matrix[c + part, :256, :]
            s = dot(x_high, high) + dot(x_low, high) + dot(x_high, matrix[c + part, 256:, :])
            lanes = slice(part * 256, part * 256 + 256)
            for q in range(2):
                row = q * 128
                val[slot, q, :, lanes] = jnp.concatenate(split(s[row : row + 64]), axis=0)
                for side in range(2):
                    w = weight[2 * side + q, pl.ds(c + part, 1), :]
                    rows = slice(side * 128, side * 128 + 128)
                    con[slot, q, rows, lanes] = jnp.concatenate(
                        split(s[row + 64 : row + 128] * w), axis=0
                    )

    def contract(slot):
        for q in range(2):
            acc[q] += dot_t(con[slot, q], val[slot, q])

    def four_groups(t, carry):
        spectra(4 * t + 2, 1)
        contract(0)
        spectra(4 * t + 4, 0)
        contract(1)
        return carry

    pieces[0].wait()
    spectra(0, 0)
    pieces[1].wait()
    lax.fori_loop(0, GROUPS // 4 - 1, four_groups, 0)
    spectra(GROUPS - 2, 1)
    contract(0)
    contract(1)

    lane = lax.broadcasted_iota(jnp.int32, (64, 128), 1)
    results = []
    for side in range(2):
        twice = []
        for q in range(2):
            part = acc[q, side * 128 : side * 128 + 64, :]
            part = part + acc[q, side * 128 + 64 : side * 128 + 128, :]
            twice.append(part + pltpu.roll(part, 64, 1))
        high, low = split(blocks_moved(jnp.where(lane < 64, twice[0], twice[1])))
        results.append(dot_t(columns[side], high) + dot_t(columns[side], low))

    first, full = results
    lane = lax.broadcasted_iota(jnp.int32, (128, 128), 1)
    down = pltpu.roll(full, 4, 0)
    even = jnp.where(lane < 64, down, pltpu.roll(full, 64, 1))
    odd = jnp.where(lane < 64, pltpu.roll(down, 64, 1), full)
    first = first.reshape(16, 8, 128)
    for i in range(32):
        out[i // 8, i % 8, :4, :] = first[i // 2, i % 2 * 4 : i % 2 * 4 + 4, :]
    zone = place[0] // 4
    turn = jnp.where(zone == 0, TURNS[0], jnp.where(zone == 3, TURNS[3], 0))
    for i in range(32):
        spot = jnp.bitwise_and(i // 8 + turn, 3)
        value = (even, odd)[i % 2][i // 2 * 8 + 4 : i // 2 * 8 + 8, :]
        out[spot, (i // 2 + 2) % 4 * 2 + i % 2, 4:, :] = value


def make_weight(screen, plane_map, planes, points):
    chosen = screen * (1.0 / (planes * points))
    group = jnp.arange(GROUPS + 1, dtype=jnp.int32)[:, None]
    other = points - plane_map
    direct = (plane_map % OUTER)[None, :] == group
    mirror = ((other % OUTER)[None, :] == group) & (other != plane_map)[None, :]
    mask = jnp.concatenate([direct, mirror], axis=1).astype(F32)
    left = mask[None] * jnp.concatenate([chosen, chosen], axis=1)[:, None, :]
    spot = jnp.concatenate([plane_map // OUTER, other // OUTER])
    right = (spot[None, :] == jnp.arange(INNER, dtype=jnp.int32)[:, None]).astype(F32)
    full = jnp.einsum("qcg,hg->qch", left, right, precision=lax.Precision.HIGHEST)
    even, middle = full[:, 0], full[:, GROUPS, : INNER // 2]
    edge = [even[:, : INNER // 2 + 1], even[:, 1 : INNER // 2], middle, middle]
    rest = full[:, 1:GROUPS]
    rest = jnp.concatenate([rest, rest], axis=2)
    return jnp.concatenate([jnp.concatenate(edge, axis=1)[:, None], rest], axis=1)


VMEM = pl.BlockSpec(memory_space=pltpu.VMEM)
SMEM = pl.BlockSpec(memory_space=pltpu.SMEM)


def call_kernel(
    body, name, *inputs, outs, scalars=0, far=(), scratch=(), limit=16, call=pl.pallas_call
):
    specs = [SMEM] * scalars + [VMEM] * (len(inputs) - scalars)
    inputs = list(inputs)
    for i in far:
        specs[i] = pl.BlockSpec(memory_space=pltpu.HBM)
        inputs[i] = pltpu.with_memory_space_constraint(inputs[i], pltpu.HBM)
    return call(
        body,
        out_shape=outs,
        in_specs=specs,
        out_specs=jax.tree.map(lambda _: VMEM, outs),
        scratch_shapes=scratch,
        compiler_params=pltpu.CompilerParams(vmem_limit_bytes=limit << 20),
        name=name,
    )(*inputs)


def make_turns(call=pl.pallas_call):
    return call_kernel(
        turns_kernel,
        "turns",
        *constants(),
        outs=jax.ShapeDtypeStruct((GROUPS, 512, 256), BF),
        call=call,
    )


def local_blocks(pair, place, data, slab, screens, turns, call=pl.pallas_call):
    return call_kernel(
        block_kernel,
        "pair_blocks",
        pair,
        place,
        data,
        slab,
        screens,
        turns,
        orders(),
        scalars=2,
        outs=jax.ShapeDtypeStruct((4, 8, 8, 128), F32),
        scratch=[
            pltpu.VMEM((OUTER, 48, INNER), F32),
            pltpu.VMEM((GROUPS, 256, 2 * INNER), F32),
            pltpu.VMEM((2, 2, 128, 512), BF),
            pltpu.VMEM((2, 2, 256, 512), BF),
            pltpu.VMEM((2, 256, 128), F32),
            pltpu.VMEM((4, GROUPS, 2 * INNER), F32),
            pltpu.VMEM((2, 128, 128), BF),
            pltpu.VMEM((GROUPS, 512, 256), BF),
            pltpu.SemaphoreType.DMA((2,)),
        ],
        far=(5,),
        limit=32,
        call=call,
    )


def shards(waves, screen, pair_table, plane_map, trial, probe):
    n_rows = lax.axis_size("ka")
    n_cols = lax.axis_size("kp")
    pair = pair_table.reshape(2)
    place = lax.axis_index("ka").astype(jnp.int32).reshape(1)

    out = call_kernel(
        first_kernel,
        "first",
        pair,
        waves.reshape(32, INNER),
        trial.reshape(64, 8).T,
        probe.transpose(0, 2, 1).reshape(8, 64),
        far=range(4),
        outs=jax.ShapeDtypeStruct((n_rows, SLAB, 128), BF),
        scratch=[
            pltpu.SMEM((2,), jnp.int32),
            pltpu.VMEM((32, 128), BF),
            pltpu.VMEM((8, 64), BF),
            pltpu.VMEM((8, 64), BF),
            pltpu.SemaphoreType.DMA((4,)),
        ],
    )
    slab = lax.all_to_all(out, "ka", 0, 0, tiled=True)
    out = call_kernel(
        second_kernel,
        "second",
        place,
        slab,
        scalars=1,
        outs=jax.ShapeDtypeStruct((n_cols, BLOCK, 128), BF),
    )
    data = lax.all_to_all(out, "kp", 0, 0, tiled=True)

    screens = make_weight(screen, plane_map, plane_map.shape[0], OUTER * INNER)
    out = local_blocks(pair, place, data, slab, screens, make_turns())

    parts = lax.all_to_all(out.reshape(n_cols, 8, 128), "kp", 0, 0, tiled=True)
    swap = []
    for a in range(n_rows):
        for b in range(n_rows):
            for c in range(2):
                spot = (b // 4 + TURNS[a // 4]) % 4 * 8 + (b + 2) % 4 * 2 + c
                swap.append((a * n_cols + spot, b * n_cols + 2 * a + c))
    adjoint = lax.ppermute(parts[:, 4:].sum(axis=0), ("ka", "kp"), swap)
    adjoint = call_kernel(last_kernel, "last", adjoint, outs=jax.ShapeDtypeStruct((8, 64), F32))
    applied = parts[:, :4].sum(axis=0).reshape(4, 2, 64)
    return applied.transpose(1, 2, 0), adjoint.T.reshape(1, 64, 8)


def solution(mesh):
    placed = (
        P("ka", None, "kp"),
        P(),
        P("ka", "kp"),
        P(),
        P("kp", None, "ka"),
        P("ka", None, "kp"),
    )
    return jax.shard_map(
        shards,
        mesh=mesh,
        in_specs=placed,
        out_specs=(P("ka", None, "kp"), P("kp", None, "ka")),
        check_vma=False,
    )
```

```python
import math

import jax
import jax.numpy as jnp
import numpy as np
from jax import lax
from jax.experimental import pallas as pl
from jax.experimental.pallas import tpu as pltpu
from jax.sharding import PartitionSpec as P

NV = 8
NC = 8
OUTER = 32
INNER = 128
BLOCK = 13
SLAB = 11
GROUPS = OUTER // 2
UNROLL = 4
TURNS = (1, 0, 0, 3)
BF = jnp.bfloat16
F32 = jnp.float32


def split_np(values):
    high = np.asarray(values, np.float32).astype(jnp.bfloat16)
    low = (np.asarray(values, np.float64) - high.astype(np.float64)).astype(jnp.bfloat16)
    return high, low


def constants():
    points = OUTER * INNER
    inner = np.arange(INNER)

    def angle(frequency):
        return 2.0 * np.pi * ((inner[:, None] * frequency[None, :]) % points) / points

    base = angle(OUTER * inner)
    group = angle(np.arange(GROUPS))
    turns = np.concatenate([np.cos(group), np.sin(group), np.zeros((INNER, 96))], axis=1)
    even = OUTER * np.arange(INNER // 2 + 1)
    middle = GROUPS + OUTER * np.arange(INNER // 2)
    zero = np.zeros((INNER, INNER))
    edge = np.block(
        [
            [np.cos(angle(even)), -np.sin(angle(even[1:-1])), zero],
            [zero, np.cos(angle(middle)), -np.sin(angle(middle))],
        ]
    )
    return (
        np.stack([np.cos(base), np.sin(base)]).astype(np.float32),
        turns.astype(np.float32),
        np.concatenate(split_np(edge), axis=0),
    )


def orders():
    order = np.zeros((2, 128, 128), np.float32)
    for spot in range(64):
        for side in range(2):
            order[side, side * 64 + spot, spot % 8 * 8 + spot // 8] = 1.0
    return order.astype(jnp.bfloat16)


def real_fft(x):
    n = len(x)
    if n == 2:
        return [x[0] + x[1], x[0] - x[1]], [None, None]
    even_re, even_im = real_fft(x[0::2])
    odd_re, odd_im = real_fft(x[1::2])
    half = n // 2
    out_re, out_im = [None] * (half + 1), [None] * (half + 1)
    out_re[0] = even_re[0] + odd_re[0]
    out_re[half] = even_re[0] - odd_re[0]
    out_re[half // 2] = even_re[half // 2]
    out_im[half // 2] = -odd_re[half // 2]
    for k in range(1, half // 2):
        c, s = math.cos(2 * math.pi * k / n), math.sin(2 * math.pi * k / n)
        if 8 * k == n:
            turn_re = (odd_re[k] + odd_im[k]) * c
            turn_im = (odd_im[k] - odd_re[k]) * c
        else:
            turn_re = odd_re[k] * c + odd_im[k] * s
            turn_im = odd_im[k] * c - odd_re[k] * s
        out_re[k] = even_re[k] + turn_re
        out_im[k] = even_im[k] + turn_im
        out_re[half - k] = even_re[k] - turn_re
        out_im[half - k] = turn_im - even_im[k]
    return out_re, out_im


def split(x):
    high = x.astype(BF)
    return high, (x - high.astype(F32)).astype(BF)


def dot(a, b):
    return lax.dot_general(a, b, (((1,), (0,)), ((), ())), preferred_element_type=F32)


def dot_t(a, b):
    return lax.dot_general(a, b, (((1,), (1,)), ((), ())), preferred_element_type=F32)


def first_kernel(pair, own, trial, probe, out, pair_here, own_here, trial_here, probe_here, sems):
    copies = [
        pltpu.make_async_copy(source, target, sems.at[i])
        for i, (source, target) in enumerate(
            ((pair, pair_here), (own, own_here), (trial, trial_here), (probe, probe_here))
        )
    ]
    for copy in copies:
        copy.start()
    for copy in copies:
        copy.wait()
    side = jnp.concatenate([trial_here[...], probe_here[...]], axis=1)
    spot = lax.broadcasted_iota(jnp.int32, (4, 128), 0)
    index = jnp.where(spot == 0, pair_here[0], pair_here[1]).astype(F32).astype(BF)
    rows = [own_here[4 * i : 4 * i + 4, :] for i in range(8)] + [side[:4], side[4:], index]
    for i in range(out.shape[0]):
        out[i, :, :] = rows[i % SLAB]


def turns_kernel(base, turns, edge, out):
    out[0] = edge[...]
    for c in range(1, GROUPS):
        cos = jnp.broadcast_to(turns[:, c : c + 1], (INNER, INNER))
        sin = jnp.broadcast_to(turns[:, GROUPS + c : GROUPS + c + 1], (INNER, INNER))
        near = split(base[0] * cos - base[1] * sin)
        far = base[1] * cos + base[0] * sin
        back = split(-far)
        far = split(far)
        for level in range(2):
            low, high = level * 256, level * 256 + 128
            out[c, low:high, :128] = near[level]
            out[c, low:high, 128:] = back[level]
            out[c, high : high + 128, :128] = far[level]
            out[c, high : high + 128, 128:] = near[level]


def second_kernel(place, slab, out):
    own = slab[pl.ds(place[0] * SLAB, 8)]
    lane = lax.broadcasted_iota(jnp.int32, (4, 128), 1)
    for i in range(out.shape[0] // BLOCK):
        half, start = i % 2, i // 2 * SLAB
        index = slab[start + 10].astype(F32)[half : half + 1]
        index = jnp.broadcast_to(index, (4, 128))
        last = jnp.where(lane < 64, index, slab[start + 8 + half].astype(F32))
        out[i * BLOCK : i * BLOCK + 8] = own
        out[i * BLOCK + 8 : i * BLOCK + 12] = slab[start + half * 4 : start + half * 4 + 4]
        out[i * BLOCK + 12] = last.astype(BF)


def last_kernel(block, out):
    out[:4, :] = block[:, :64]
    out[4:, :] = block[:, 64:]


def blocks_moved(both):
    spot = lax.broadcasted_iota(jnp.int32, (8, 128), 1) // 8 % 8
    rows = []
    for new in range(8):
        row = jnp.zeros((8, 128), F32)
        for old in range(8):
            block = both[old * 8 : old * 8 + 8]
            shift = (old - new) * 8 % 128
            if shift:
                block = pltpu.roll(block, shift, 1)
            row = jnp.where(spot == old, block, row)
        rows.append(row)
    moved = jnp.concatenate(rows, axis=0)
    return jnp.concatenate([moved, pltpu.roll(moved, 64, 1)], axis=0)


def block_kernel(
    pair,
    place,
    data,
    slab,
    screens,
    turns,
    order,
    out,
    wide,
    grid,
    val,
    con,
    acc,
    weight,
    columns,
    matrix,
    sems,
):
    def piece(i):
        part = pl.ds(2 * i, 2)
        return pltpu.make_async_copy(turns.at[part], matrix.at[part], sems.at[i])

    for i in range(GROUPS // 2):
        piece(i).start()
    parts = data[...].reshape(OUTER, BLOCK, 4, 128)
    for i in range(12):
        wide[:, 4 * i : 4 * i + 4, :] = parts[:, i].astype(F32)
    for q in range(2):
        weight[q] = screens[pair[q]]
        other = data[(2 * place[0] + q) * BLOCK + 12].astype(F32)[:, :64]
        weight[2 + q] = screens[jnp.max(other).astype(jnp.int32)]

    def transform(i):
        q, t, s = i // 16, i // 8 % 2, i % 8
        single = (1 - t) * (q * 16) + t * 40 + s
        side = pl.multiple_of((1 - t) * 32 + t * (q * 16 + 8), 8)
        base = pl.multiple_of(i * 8, 8)
        tiles = [
            jnp.broadcast_to(wide[a, pl.ds(single, 1), :], (8, INNER)) * wide[a, pl.ds(side, 8), :]
            for a in range(OUTER)
        ]
        re, im = real_fft(tiles)
        grid[0, pl.ds(base, 8), :INNER] = re[0]
        grid[0, pl.ds(base, 8), INNER:] = re[GROUPS]
        for c in range(1, GROUPS):
            grid[c, pl.ds(base, 8), :INNER] = re[c]
            grid[c, pl.ds(base, 8), INNER:] = im[c]

    def transform_some(i, carry):
        for part in range(UNROLL):
            transform(i * UNROLL + part)
        return carry

    lax.fori_loop(0, 32 // UNROLL, transform_some, 0)
    acc[...] = jnp.zeros_like(acc)
    side = slab[...].reshape(16, SLAB, 4, 128)[:, 8:10].reshape(128, 128)
    inputs = (side, parts[:, 12].reshape(128, 128))
    for side in range(2):
        columns[side] = dot(inputs[side].astype(BF), order[side]).astype(BF)

    def spectra(c, slot):
        for part in range(2):
            x_high, x_low = split(grid[c + part])
            high = matrix[c + part, :256, :]
            s = dot(x_high, high) + dot(x_low, high) + dot(x_high, matrix[c + part, 256:, :])
            lanes = slice(part * 256, part * 256 + 256)
            for q in range(2):
                row = q * 128
                val[slot, q, :, lanes] = jnp.concatenate(split(s[row : row + 64]), axis=0)
                for side in range(2):
                    w = weight[2 * side + q, pl.ds(c + part, 1), :]
                    rows = slice(side * 128, side * 128 + 128)
                    con[slot, q, rows, lanes] = jnp.concatenate(
                        split(s[row + 64 : row + 128] * w), axis=0
                    )

    def contract(slot):
        for q in range(2):
            acc[q] += dot_t(con[slot, q], val[slot, q])

    def four_groups(t, carry):
        piece(2 * t + 1).wait()
        piece(2 * t + 2).wait()
        spectra(4 * t + 2, 1)
        contract(0)
        spectra(4 * t + 4, 0)
        contract(1)
        return carry

    piece(0).wait()
    spectra(0, 0)
    lax.fori_loop(0, GROUPS // 4 - 1, four_groups, 0)
    piece(GROUPS // 2 - 1).wait()
    spectra(GROUPS - 2, 1)
    contract(0)
    contract(1)

    lane = lax.broadcasted_iota(jnp.int32, (64, 128), 1)
    results = []
    for side in range(2):
        twice = []
        for q in range(2):
            part = acc[q, side * 128 : side * 128 + 64, :]
            part = part + acc[q, side * 128 + 64 : side * 128 + 128, :]
            twice.append(part + pltpu.roll(part, 64, 1))
        high, low = split(blocks_moved(jnp.where(lane < 64, twice[0], twice[1])))
        results.append(dot_t(columns[side], high) + dot_t(columns[side], low))

    first, full = results
    lane = lax.broadcasted_iota(jnp.int32, (128, 128), 1)
    down = pltpu.roll(full, 4, 0)
    even = jnp.where(lane < 64, down, pltpu.roll(full, 64, 1))
    odd = jnp.where(lane < 64, pltpu.roll(down, 64, 1), full)
    first = first.reshape(16, 8, 128)
    for i in range(32):
        out[i // 8, i % 8, :4, :] = first[i // 2, i % 2 * 4 : i % 2 * 4 + 4, :]
    zone = place[0] // 4
    turn = jnp.where(zone == 0, TURNS[0], jnp.where(zone == 3, TURNS[3], 0))
    for i in range(32):
        spot = jnp.bitwise_and(i // 8 + turn, 3)
        value = (even, odd)[i % 2][i // 2 * 8 + 4 : i // 2 * 8 + 8, :]
        out[spot, (i // 2 + 2) % 4 * 2 + i % 2, 4:, :] = value


def make_weight(screen, plane_map, planes, points):
    chosen = screen * (1.0 / (planes * points))
    group = jnp.arange(GROUPS + 1, dtype=jnp.int32)[:, None]
    other = points - plane_map
    direct = (plane_map % OUTER)[None, :] == group
    mirror = ((other % OUTER)[None, :] == group) & (other != plane_map)[None, :]
    mask = jnp.concatenate([direct, mirror], axis=1).astype(F32)
    left = mask[None] * jnp.concatenate([chosen, chosen], axis=1)[:, None, :]
    spot = jnp.concatenate([plane_map // OUTER, other // OUTER])
    right = (spot[None, :] == jnp.arange(INNER, dtype=jnp.int32)[:, None]).astype(F32)
    full = jnp.einsum("qcg,hg->qch", left, right, precision=lax.Precision.HIGHEST)
    even, middle = full[:, 0], full[:, GROUPS, : INNER // 2]
    edge = [even[:, : INNER // 2 + 1], even[:, 1 : INNER // 2], middle, middle]
    rest = full[:, 1:GROUPS]
    rest = jnp.concatenate([rest, rest], axis=2)
    return jnp.concatenate([jnp.concatenate(edge, axis=1)[:, None], rest], axis=1)


VMEM = pl.BlockSpec(memory_space=pltpu.VMEM)
SMEM = pl.BlockSpec(memory_space=pltpu.SMEM)


def call_kernel(
    body, name, *inputs, outs, scalars=0, far=(), scratch=(), limit=16, call=pl.pallas_call
):
    specs = [SMEM] * scalars + [VMEM] * (len(inputs) - scalars)
    inputs = list(inputs)
    for i in far:
        specs[i] = pl.BlockSpec(memory_space=pltpu.HBM)
        inputs[i] = pltpu.with_memory_space_constraint(inputs[i], pltpu.HBM)
    return call(
        body,
        out_shape=outs,
        in_specs=specs,
        out_specs=jax.tree.map(lambda _: VMEM, outs),
        scratch_shapes=scratch,
        compiler_params=pltpu.CompilerParams(vmem_limit_bytes=limit << 20),
        name=name,
    )(*inputs)


def make_turns(call=pl.pallas_call):
    return call_kernel(
        turns_kernel,
        "turns",
        *constants(),
        outs=jax.ShapeDtypeStruct((GROUPS, 512, 256), BF),
        call=call,
    )


def local_blocks(pair, place, data, slab, screens, turns, call=pl.pallas_call):
    return call_kernel(
        block_kernel,
        "pair_blocks",
        pair,
        place,
        data,
        slab,
        screens,
        turns,
        orders(),
        scalars=2,
        outs=jax.ShapeDtypeStruct((4, 8, 8, 128), F32),
        scratch=[
            pltpu.VMEM((OUTER, 48, INNER), F32),
            pltpu.VMEM((GROUPS, 256, 2 * INNER), F32),
            pltpu.VMEM((2, 2, 128, 512), BF),
            pltpu.VMEM((2, 2, 256, 512), BF),
            pltpu.VMEM((2, 256, 128), F32),
            pltpu.VMEM((4, GROUPS, 2 * INNER), F32),
            pltpu.VMEM((2, 128, 128), BF),
            pltpu.VMEM((GROUPS, 512, 256), BF),
            pltpu.SemaphoreType.DMA((GROUPS // 2,)),
        ],
        far=(5,),
        limit=32,
        call=call,
    )


def shards(waves, screen, pair_table, plane_map, trial, probe):
    n_rows = lax.axis_size("ka")
    n_cols = lax.axis_size("kp")
    pair = pair_table.reshape(2)
    place = lax.axis_index("ka").astype(jnp.int32).reshape(1)

    out = call_kernel(
        first_kernel,
        "first",
        pair,
        waves.reshape(32, INNER),
        trial.reshape(64, 8).T,
        probe.transpose(0, 2, 1).reshape(8, 64),
        far=range(4),
        outs=jax.ShapeDtypeStruct((n_rows * SLAB, 4, 128), BF),
        scratch=[
            pltpu.SMEM((2,), jnp.int32),
            pltpu.VMEM((32, 128), BF),
            pltpu.VMEM((8, 64), BF),
            pltpu.VMEM((8, 64), BF),
            pltpu.SemaphoreType.DMA((4,)),
        ],
    )
    slab = lax.all_to_all(out, "ka", 0, 0, tiled=True)
    out = call_kernel(
        second_kernel,
        "second",
        place,
        slab,
        scalars=1,
        outs=jax.ShapeDtypeStruct((n_cols * BLOCK, 4, 128), BF),
    )
    data = lax.all_to_all(out, "kp", 0, 0, tiled=True)

    screens = make_weight(screen, plane_map, plane_map.shape[0], OUTER * INNER)
    out = local_blocks(pair, place, data, slab, screens, make_turns())

    parts = lax.all_to_all(out.reshape(n_cols, 8, 128), "kp", 0, 0, tiled=True)
    swap = []
    for a in range(n_rows):
        for b in range(n_rows):
            for c in range(2):
                spot = (b // 4 + TURNS[a // 4]) % 4 * 8 + (b + 2) % 4 * 2 + c
                swap.append((a * n_cols + spot, b * n_cols + 2 * a + c))
    adjoint = lax.ppermute(parts[:, 4:].sum(axis=0), ("ka", "kp"), swap)
    adjoint = call_kernel(last_kernel, "last", adjoint, outs=jax.ShapeDtypeStruct((8, 64), F32))
    applied = parts[:, :4].sum(axis=0).reshape(4, 2, 64)
    return applied.transpose(1, 2, 0), adjoint.T.reshape(1, 64, 8)


def solution(mesh):
    placed = (
        P("ka", None, "kp"),
        P(),
        P("ka", "kp"),
        P(),
        P("kp", None, "ka"),
        P("ka", None, "kp"),
    )
    return jax.shard_map(
        shards,
        mesh=mesh,
        in_specs=placed,
        out_specs=(P("ka", None, "kp"), P("kp", None, "ka")),
        check_vma=False,
    )
```

```python
import math

import jax
import jax.numpy as jnp
import numpy as np
from jax import lax
from jax.experimental import pallas as pl
from jax.experimental.pallas import tpu as pltpu
from jax.sharding import PartitionSpec as P

NV = 8
NC = 8
OUTER = 32
INNER = 128
BLOCK = 13
SLAB = 11
GROUPS = OUTER // 2
UNROLL = 4
TURNS = (1, 0, 0, 3)
BF = jnp.bfloat16
F32 = jnp.float32


def split_np(values):
    high = np.asarray(values, np.float32).astype(jnp.bfloat16)
    low = (np.asarray(values, np.float64) - high.astype(np.float64)).astype(jnp.bfloat16)
    return high, low


def constants():
    points = OUTER * INNER
    inner = np.arange(INNER)

    def angle(frequency):
        return 2.0 * np.pi * ((inner[:, None] * frequency[None, :]) % points) / points

    base = angle(OUTER * inner)
    group = angle(np.arange(GROUPS))
    turns = np.concatenate([np.cos(group), np.sin(group), np.zeros((INNER, 96))], axis=1)
    even = OUTER * np.arange(INNER // 2 + 1)
    middle = GROUPS + OUTER * np.arange(INNER // 2)
    zero = np.zeros((INNER, INNER))
    edge = np.block(
        [
            [np.cos(angle(even)), -np.sin(angle(even[1:-1])), zero],
            [zero, np.cos(angle(middle)), -np.sin(angle(middle))],
        ]
    )
    return (
        np.stack([np.cos(base), np.sin(base)]).astype(np.float32),
        turns.astype(np.float32),
        np.concatenate(split_np(edge), axis=0),
    )


def orders():
    order = np.zeros((2, 128, 128), np.float32)
    for spot in range(64):
        for side in range(2):
            order[side, side * 64 + spot, spot % 8 * 8 + spot // 8] = 1.0
    return order.astype(jnp.bfloat16)


def real_fft(x):
    n = len(x)
    if n == 2:
        return [x[0] + x[1], x[0] - x[1]], [None, None]
    even_re, even_im = real_fft(x[0::2])
    odd_re, odd_im = real_fft(x[1::2])
    half = n // 2
    out_re, out_im = [None] * (half + 1), [None] * (half + 1)
    out_re[0] = even_re[0] + odd_re[0]
    out_re[half] = even_re[0] - odd_re[0]
    out_re[half // 2] = even_re[half // 2]
    out_im[half // 2] = -odd_re[half // 2]
    for k in range(1, half // 2):
        c, s = math.cos(2 * math.pi * k / n), math.sin(2 * math.pi * k / n)
        if 8 * k == n:
            turn_re = (odd_re[k] + odd_im[k]) * c
            turn_im = (odd_im[k] - odd_re[k]) * c
        else:
            turn_re = odd_re[k] * c + odd_im[k] * s
            turn_im = odd_im[k] * c - odd_re[k] * s
        out_re[k] = even_re[k] + turn_re
        out_im[k] = even_im[k] + turn_im
        out_re[half - k] = even_re[k] - turn_re
        out_im[half - k] = turn_im - even_im[k]
    return out_re, out_im


def split(x):
    high = x.astype(BF)
    return high, (x - high.astype(F32)).astype(BF)


def dot(a, b):
    return lax.dot_general(a, b, (((1,), (0,)), ((), ())), preferred_element_type=F32)


def dot_t(a, b):
    return lax.dot_general(a, b, (((1,), (1,)), ((), ())), preferred_element_type=F32)


def first_kernel(pair, own, trial, probe, out, pair_here, own_here, trial_here, probe_here, sems):
    copies = [
        pltpu.make_async_copy(source, target, sems.at[i])
        for i, (source, target) in enumerate(
            ((pair, pair_here), (own, own_here), (trial, trial_here), (probe, probe_here))
        )
    ]
    for copy in copies:
        copy.start()
    for copy in copies:
        copy.wait()
    side = jnp.concatenate([trial_here[...], probe_here[...]], axis=1)
    spot = lax.broadcasted_iota(jnp.int32, (4, 128), 0)
    index = jnp.where(spot == 0, pair_here[0], pair_here[1]).astype(F32).astype(BF)
    rows = [own_here[4 * i : 4 * i + 4, :] for i in range(8)] + [side[:4], side[4:], index]
    for i in range(out.shape[0]):
        out[i, :, :] = rows[i % SLAB]


def turns_kernel(base, turns, edge, out):
    out[0] = edge[...]
    for c in range(1, GROUPS):
        cos = jnp.broadcast_to(turns[:, c : c + 1], (INNER, INNER))
        sin = jnp.broadcast_to(turns[:, GROUPS + c : GROUPS + c + 1], (INNER, INNER))
        near = split(base[0] * cos - base[1] * sin)
        far = base[1] * cos + base[0] * sin
        back = split(-far)
        far = split(far)
        for level in range(2):
            low, high = level * 256, level * 256 + 128
            out[c, low:high, :128] = near[level]
            out[c, low:high, 128:] = back[level]
            out[c, high : high + 128, :128] = far[level]
            out[c, high : high + 128, 128:] = near[level]


def second_kernel(slab, out):
    own = slab[pl.ds(lax.axis_index("ka") * SLAB, 8)]
    lane = lax.broadcasted_iota(jnp.int32, (4, 128), 1)
    for i in range(out.shape[0] // BLOCK):
        half, start = i % 2, i // 2 * SLAB
        index = slab[start + 10].astype(F32)[half : half + 1]
        index = jnp.broadcast_to(index, (4, 128))
        last = jnp.where(lane < 64, index, slab[start + 8 + half].astype(F32))
        out[i * BLOCK : i * BLOCK + 8] = own
        out[i * BLOCK + 8 : i * BLOCK + 12] = slab[start + half * 4 : start + half * 4 + 4]
        out[i * BLOCK + 12] = last.astype(BF)


def last_kernel(block, out):
    out[:4, :] = block[:, :64]
    out[4:, :] = block[:, 64:]


def blocks_moved(both):
    spot = lax.broadcasted_iota(jnp.int32, (8, 128), 1) // 8 % 8
    rows = []
    for new in range(8):
        row = jnp.zeros((8, 128), F32)
        for old in range(8):
            block = both[old * 8 : old * 8 + 8]
            shift = (old - new) * 8 % 128
            if shift:
                block = pltpu.roll(block, shift, 1)
            row = jnp.where(spot == old, block, row)
        rows.append(row)
    moved = jnp.concatenate(rows, axis=0)
    return jnp.concatenate([moved, pltpu.roll(moved, 64, 1)], axis=0)


def block_kernel(
    pair,
    data,
    slab,
    screens,
    turns,
    order,
    out,
    wide,
    grid,
    val,
    con,
    acc,
    weight,
    columns,
    matrix,
    sems,
):
    def piece(i):
        part = pl.ds(2 * i, 2)
        return pltpu.make_async_copy(turns.at[part], matrix.at[part], sems.at[i])

    for i in range(GROUPS // 2):
        piece(i).start()
    parts = data[...].reshape(OUTER, BLOCK, 4, 128)
    for i in range(12):
        wide[:, 4 * i : 4 * i + 4, :] = parts[:, i].astype(F32)
    for q in range(2):
        weight[q] = screens[pair[q]]
        other = data[(2 * lax.axis_index("ka") + q) * BLOCK + 12].astype(F32)[:, :64]
        weight[2 + q] = screens[jnp.max(other).astype(jnp.int32)]

    def transform(i):
        q, t, s = i // 16, i // 8 % 2, i % 8
        single = (1 - t) * (q * 16) + t * 40 + s
        side = pl.multiple_of((1 - t) * 32 + t * (q * 16 + 8), 8)
        base = pl.multiple_of(i * 8, 8)
        tiles = [
            jnp.broadcast_to(wide[a, pl.ds(single, 1), :], (8, INNER)) * wide[a, pl.ds(side, 8), :]
            for a in range(OUTER)
        ]
        re, im = real_fft(tiles)
        grid[0, pl.ds(base, 8), :INNER] = re[0]
        grid[0, pl.ds(base, 8), INNER:] = re[GROUPS]
        for c in range(1, GROUPS):
            grid[c, pl.ds(base, 8), :INNER] = re[c]
            grid[c, pl.ds(base, 8), INNER:] = im[c]

    def transform_some(i, carry):
        for part in range(UNROLL):
            transform(i * UNROLL + part)
        return carry

    lax.fori_loop(0, 32 // UNROLL, transform_some, 0)
    acc[...] = jnp.zeros_like(acc)
    side = slab[...].reshape(16, SLAB, 4, 128)[:, 8:10].reshape(128, 128)
    inputs = (side, parts[:, 12].reshape(128, 128))
    for side in range(2):
        columns[side] = dot(inputs[side].astype(BF), order[side]).astype(BF)

    def spectra(c, slot):
        for part in range(2):
            x_high, x_low = split(grid[c + part])
            high = matrix[c + part, :256, :]
            s = dot(x_high, high) + dot(x_low, high) + dot(x_high, matrix[c + part, 256:, :])
            lanes = slice(part * 256, part * 256 + 256)
            for q in range(2):
                row = q * 128
                val[slot, q, :, lanes] = jnp.concatenate(split(s[row : row + 64]), axis=0)
                for side in range(2):
                    w = weight[2 * side + q, pl.ds(c + part, 1), :]
                    rows = slice(side * 128, side * 128 + 128)
                    con[slot, q, rows, lanes] = jnp.concatenate(
                        split(s[row + 64 : row + 128] * w), axis=0
                    )

    def contract(slot):
        for q in range(2):
            acc[q] += dot_t(con[slot, q], val[slot, q])

    def four_groups(t, carry):
        piece(2 * t + 1).wait()
        piece(2 * t + 2).wait()
        spectra(4 * t + 2, 1)
        contract(0)
        spectra(4 * t + 4, 0)
        contract(1)
        return carry

    piece(0).wait()
    spectra(0, 0)
    lax.fori_loop(0, GROUPS // 4 - 1, four_groups, 0)
    piece(GROUPS // 2 - 1).wait()
    spectra(GROUPS - 2, 1)
    contract(0)
    contract(1)

    lane = lax.broadcasted_iota(jnp.int32, (64, 128), 1)
    results = []
    for side in range(2):
        twice = []
        for q in range(2):
            part = acc[q, side * 128 : side * 128 + 64, :]
            part = part + acc[q, side * 128 + 64 : side * 128 + 128, :]
            twice.append(part + pltpu.roll(part, 64, 1))
        high, low = split(blocks_moved(jnp.where(lane < 64, twice[0], twice[1])))
        results.append(dot_t(columns[side], high) + dot_t(columns[side], low))

    first, full = results
    lane = lax.broadcasted_iota(jnp.int32, (128, 128), 1)
    down = pltpu.roll(full, 4, 0)
    even = jnp.where(lane < 64, down, pltpu.roll(full, 64, 1))
    odd = jnp.where(lane < 64, pltpu.roll(down, 64, 1), full)
    first = first.reshape(16, 8, 128)
    for i in range(32):
        out[i // 8, i % 8, :4, :] = first[i // 2, i % 2 * 4 : i % 2 * 4 + 4, :]
    zone = lax.axis_index("ka") // 4
    turn = jnp.where(zone == 0, TURNS[0], jnp.where(zone == 3, TURNS[3], 0))
    for i in range(32):
        spot = jnp.bitwise_and(i // 8 + turn, 3)
        value = (even, odd)[i % 2][i // 2 * 8 + 4 : i // 2 * 8 + 8, :]
        out[spot, (i // 2 + 2) % 4 * 2 + i % 2, 4:, :] = value


def make_weight(screen, plane_map, planes, points):
    chosen = screen * (1.0 / (planes * points))
    group = jnp.arange(GROUPS + 1, dtype=jnp.int32)[:, None]
    other = points - plane_map
    direct = (plane_map % OUTER)[None, :] == group
    mirror = ((other % OUTER)[None, :] == group) & (other != plane_map)[None, :]
    mask = jnp.concatenate([direct, mirror], axis=1).astype(F32)
    left = mask[None] * jnp.concatenate([chosen, chosen], axis=1)[:, None, :]
    spot = jnp.concatenate([plane_map // OUTER, other // OUTER])
    right = (spot[None, :] == jnp.arange(INNER, dtype=jnp.int32)[:, None]).astype(F32)
    full = jnp.einsum("qcg,hg->qch", left, right, precision=lax.Precision.HIGHEST)
    even, middle = full[:, 0], full[:, GROUPS, : INNER // 2]
    edge = [even[:, : INNER // 2 + 1], even[:, 1 : INNER // 2], middle, middle]
    rest = full[:, 1:GROUPS]
    rest = jnp.concatenate([rest, rest], axis=2)
    return jnp.concatenate([jnp.concatenate(edge, axis=1)[:, None], rest], axis=1)


VMEM = pl.BlockSpec(memory_space=pltpu.VMEM)
SMEM = pl.BlockSpec(memory_space=pltpu.SMEM)


def call_kernel(
    body, name, *inputs, outs, scalars=0, far=(), scratch=(), limit=16, call=pl.pallas_call
):
    specs = [SMEM] * scalars + [VMEM] * (len(inputs) - scalars)
    inputs = list(inputs)
    for i in far:
        specs[i] = pl.BlockSpec(memory_space=pltpu.HBM)
        inputs[i] = pltpu.with_memory_space_constraint(inputs[i], pltpu.HBM)
    return call(
        body,
        out_shape=outs,
        in_specs=specs,
        out_specs=jax.tree.map(lambda _: VMEM, outs),
        scratch_shapes=scratch,
        compiler_params=pltpu.CompilerParams(vmem_limit_bytes=limit << 20),
        name=name,
    )(*inputs)


def make_turns(tables, call=pl.pallas_call):
    return call_kernel(
        turns_kernel,
        "turns",
        *tables,
        outs=jax.ShapeDtypeStruct((GROUPS, 512, 256), BF),
        call=call,
    )


def local_blocks(pair, data, slab, screens, turns, call=pl.pallas_call):
    return call_kernel(
        block_kernel,
        "pair_blocks",
        pair,
        data,
        slab,
        screens,
        turns,
        orders(),
        scalars=1,
        outs=jax.ShapeDtypeStruct((4, 8, 8, 128), F32),
        scratch=[
            pltpu.VMEM((OUTER, 48, INNER), F32),
            pltpu.VMEM((GROUPS, 256, 2 * INNER), F32),
            pltpu.VMEM((2, 2, 128, 512), BF),
            pltpu.VMEM((2, 2, 256, 512), BF),
            pltpu.VMEM((2, 256, 128), F32),
            pltpu.VMEM((4, GROUPS, 2 * INNER), F32),
            pltpu.VMEM((2, 128, 128), BF),
            pltpu.VMEM((GROUPS, 512, 256), BF),
            pltpu.SemaphoreType.DMA((GROUPS // 2,)),
        ],
        far=(4,),
        limit=32,
        call=call,
    )


def shards(waves, screen, pair_table, plane_map, trial, probe):
    n_rows = lax.axis_size("ka")
    n_cols = lax.axis_size("kp")
    pair = pair_table.reshape(2)

    out = call_kernel(
        first_kernel,
        "first",
        pair,
        waves.reshape(32, INNER),
        trial.reshape(64, 8).T,
        probe.transpose(0, 2, 1).reshape(8, 64),
        far=range(4),
        outs=jax.ShapeDtypeStruct((n_rows * SLAB, 4, 128), BF),
        scratch=[
            pltpu.SMEM((2,), jnp.int32),
            pltpu.VMEM((32, 128), BF),
            pltpu.VMEM((8, 64), BF),
            pltpu.VMEM((8, 64), BF),
            pltpu.SemaphoreType.DMA((4,)),
        ],
    )
    slab = lax.all_to_all(out, "ka", 0, 0, tiled=True)
    tables = [jnp.asarray(table) for table in constants()]
    slab, plane_map, screen, tables = lax.optimization_barrier((slab, plane_map, screen, tables))
    out = call_kernel(
        second_kernel,
        "second",
        slab,
        outs=jax.ShapeDtypeStruct((n_cols * BLOCK, 4, 128), BF),
    )
    data = lax.all_to_all(out, "kp", 0, 0, tiled=True)

    screens = make_weight(screen, plane_map, plane_map.shape[0], OUTER * INNER)
    out = local_blocks(pair, data, slab, screens, make_turns(tables))

    parts = lax.all_to_all(out.reshape(n_cols, 8, 128), "kp", 0, 0, tiled=True)
    swap = []
    for a in range(n_rows):
        for b in range(n_rows):
            for c in range(2):
                spot = (b // 4 + TURNS[a // 4]) % 4 * 8 + (b + 2) % 4 * 2 + c
                swap.append((a * n_cols + spot, b * n_cols + 2 * a + c))
    adjoint = lax.ppermute(parts[:, 4:].sum(axis=0), ("ka", "kp"), swap)
    adjoint = call_kernel(last_kernel, "last", adjoint, outs=jax.ShapeDtypeStruct((8, 64), F32))
    applied = parts[:, :4].sum(axis=0).reshape(4, 2, 64)
    return applied.transpose(1, 2, 0), adjoint.T.reshape(1, 64, 8)


def solution(mesh):
    placed = (
        P("ka", None, "kp"),
        P(),
        P("ka", "kp"),
        P(),
        P("kp", None, "ka"),
        P("ka", None, "kp"),
    )
    return jax.shard_map(
        shards,
        mesh=mesh,
        in_specs=placed,
        out_specs=(P("ka", None, "kp"), P("kp", None, "ka")),
        check_vma=False,
    )
```

```python
import math

import jax
import jax.numpy as jnp
import numpy as np
from jax import lax
from jax.experimental import pallas as pl
from jax.experimental.pallas import tpu as pltpu
from jax.sharding import PartitionSpec as P

NV = 8
NC = 8
OUTER = 32
INNER = 128
BLOCK = 13
SLAB = 11
GROUPS = OUTER // 2
UNROLL = 4
TURNS = (1, 0, 0, 3)
BF = jnp.bfloat16
F32 = jnp.float32


def split_np(values):
    high = np.asarray(values, np.float32).astype(jnp.bfloat16)
    low = (np.asarray(values, np.float64) - high.astype(np.float64)).astype(jnp.bfloat16)
    return high, low


def constants():
    points = OUTER * INNER
    inner = np.arange(INNER)

    def angle(frequency):
        return 2.0 * np.pi * ((inner[:, None] * frequency[None, :]) % points) / points

    base = angle(OUTER * inner)
    group = angle(np.arange(GROUPS))
    turns = np.concatenate([np.cos(group), np.sin(group), np.zeros((INNER, 96))], axis=1)
    even = OUTER * np.arange(INNER // 2 + 1)
    middle = GROUPS + OUTER * np.arange(INNER // 2)
    zero = np.zeros((INNER, INNER))
    edge = np.block(
        [
            [np.cos(angle(even)), -np.sin(angle(even[1:-1])), zero],
            [zero, np.cos(angle(middle)), -np.sin(angle(middle))],
        ]
    )
    return (
        np.stack([np.cos(base), np.sin(base)]).astype(np.float32),
        turns.astype(np.float32),
        np.concatenate(split_np(edge), axis=0),
    )


def orders():
    order = np.zeros((2, 128, 128), np.float32)
    for spot in range(64):
        for side in range(2):
            order[side, side * 64 + spot, spot % 8 * 8 + spot // 8] = 1.0
    return order.astype(jnp.bfloat16)


def real_fft(x):
    n = len(x)
    if n == 2:
        return [x[0] + x[1], x[0] - x[1]], [None, None]
    even_re, even_im = real_fft(x[0::2])
    odd_re, odd_im = real_fft(x[1::2])
    half = n // 2
    out_re, out_im = [None] * (half + 1), [None] * (half + 1)
    out_re[0] = even_re[0] + odd_re[0]
    out_re[half] = even_re[0] - odd_re[0]
    out_re[half // 2] = even_re[half // 2]
    out_im[half // 2] = -odd_re[half // 2]
    for k in range(1, half // 2):
        c, s = math.cos(2 * math.pi * k / n), math.sin(2 * math.pi * k / n)
        if 8 * k == n:
            turn_re = (odd_re[k] + odd_im[k]) * c
            turn_im = (odd_im[k] - odd_re[k]) * c
        else:
            turn_re = odd_re[k] * c + odd_im[k] * s
            turn_im = odd_im[k] * c - odd_re[k] * s
        out_re[k] = even_re[k] + turn_re
        out_im[k] = even_im[k] + turn_im
        out_re[half - k] = even_re[k] - turn_re
        out_im[half - k] = turn_im - even_im[k]
    return out_re, out_im


def split(x):
    high = x.astype(BF)
    return high, (x - high.astype(F32)).astype(BF)


def dot(a, b):
    return lax.dot_general(a, b, (((1,), (0,)), ((), ())), preferred_element_type=F32)


def dot_t(a, b):
    return lax.dot_general(a, b, (((1,), (1,)), ((), ())), preferred_element_type=F32)


def first_kernel(pair, own, trial, probe, out, pair_here, own_here, trial_here, probe_here, sems):
    copies = [
        pltpu.make_async_copy(source, target, sems.at[i])
        for i, (source, target) in enumerate(
            ((pair, pair_here), (own, own_here), (trial, trial_here), (probe, probe_here))
        )
    ]
    for copy in copies:
        copy.start()
    for copy in copies:
        copy.wait()
    side = jnp.concatenate([trial_here[...], probe_here[...]], axis=1)
    spot = lax.broadcasted_iota(jnp.int32, (4, 128), 0)
    index = jnp.where(spot == 0, pair_here[0], pair_here[1]).astype(F32).astype(BF)
    rows = [own_here[4 * i : 4 * i + 4, :] for i in range(8)] + [side[:4], side[4:], index]
    for i in range(out.shape[0]):
        out[i, :, :] = rows[i % SLAB]


def turns_kernel(base, turns, edge, out):
    out[0] = edge[...]
    for c in range(1, GROUPS):
        cos = jnp.broadcast_to(turns[:, c : c + 1], (INNER, INNER))
        sin = jnp.broadcast_to(turns[:, GROUPS + c : GROUPS + c + 1], (INNER, INNER))
        near = split(base[0] * cos - base[1] * sin)
        far = base[1] * cos + base[0] * sin
        back = split(-far)
        far = split(far)
        for level in range(2):
            low, high = level * 256, level * 256 + 128
            out[c, low:high, :128] = near[level]
            out[c, low:high, 128:] = back[level]
            out[c, high : high + 128, :128] = far[level]
            out[c, high : high + 128, 128:] = near[level]


def second_kernel(slab, out):
    own = slab[pl.ds(lax.axis_index("ka") * SLAB, 8)]
    lane = lax.broadcasted_iota(jnp.int32, (4, 128), 1)
    for i in range(out.shape[0] // BLOCK):
        half, start = i % 2, i // 2 * SLAB
        index = slab[start + 10].astype(F32)[half : half + 1]
        index = jnp.broadcast_to(index, (4, 128))
        last = jnp.where(lane < 64, index, slab[start + 8 + half].astype(F32))
        out[i * BLOCK : i * BLOCK + 8] = own
        out[i * BLOCK + 8 : i * BLOCK + 12] = slab[start + half * 4 : start + half * 4 + 4]
        out[i * BLOCK + 12] = last.astype(BF)


def last_kernel(block, out):
    out[:4, :] = block[:, :64]
    out[4:, :] = block[:, 64:]


def blocks_moved(both):
    spot = lax.broadcasted_iota(jnp.int32, (8, 128), 1) // 8 % 8
    rows = []
    for new in range(8):
        row = jnp.zeros((8, 128), F32)
        for old in range(8):
            block = both[old * 8 : old * 8 + 8]
            shift = (old - new) * 8 % 128
            if shift:
                block = pltpu.roll(block, shift, 1)
            row = jnp.where(spot == old, block, row)
        rows.append(row)
    moved = jnp.concatenate(rows, axis=0)
    return jnp.concatenate([moved, pltpu.roll(moved, 64, 1)], axis=0)


def block_kernel(
    pair,
    place,
    data,
    slab,
    screens,
    turns,
    order,
    out,
    wide,
    grid,
    val,
    con,
    acc,
    weight,
    columns,
    matrix,
    sems,
):
    def piece(i):
        part = pl.ds(2 * i, 2)
        return pltpu.make_async_copy(turns.at[part], matrix.at[part], sems.at[i])

    for i in range(GROUPS // 2):
        piece(i).start()
    parts = data[...].reshape(OUTER, BLOCK, 4, 128)
    for i in range(12):
        wide[:, 4 * i : 4 * i + 4, :] = parts[:, i].astype(F32)
    for q in range(2):
        weight[q] = screens[pair[q]]
        other = data[(2 * place[0] + q) * BLOCK + 12].astype(F32)[:, :64]
        weight[2 + q] = screens[jnp.max(other).astype(jnp.int32)]

    def transform(i):
        q, t, s = i // 16, i // 8 % 2, i % 8
        single = (1 - t) * (q * 16) + t * 40 + s
        side = pl.multiple_of((1 - t) * 32 + t * (q * 16 + 8), 8)
        base = pl.multiple_of(i * 8, 8)
        tiles = [
            jnp.broadcast_to(wide[a, pl.ds(single, 1), :], (8, INNER)) * wide[a, pl.ds(side, 8), :]
            for a in range(OUTER)
        ]
        re, im = real_fft(tiles)
        grid[0, pl.ds(base, 8), :INNER] = re[0]
        grid[0, pl.ds(base, 8), INNER:] = re[GROUPS]
        for c in range(1, GROUPS):
            grid[c, pl.ds(base, 8), :INNER] = re[c]
            grid[c, pl.ds(base, 8), INNER:] = im[c]

    def transform_some(i, carry):
        for part in range(UNROLL):
            transform(i * UNROLL + part)
        return carry

    lax.fori_loop(0, 32 // UNROLL, transform_some, 0)
    acc[...] = jnp.zeros_like(acc)
    side = slab[...].reshape(16, SLAB, 4, 128)[:, 8:10].reshape(128, 128)
    inputs = (side, parts[:, 12].reshape(128, 128))
    for side in range(2):
        columns[side] = dot(inputs[side].astype(BF), order[side]).astype(BF)

    def spectra(c, slot):
        for part in range(2):
            x_high, x_low = split(grid[c + part])
            high = matrix[c + part, :256, :]
            s = dot(x_high, high) + dot(x_low, high) + dot(x_high, matrix[c + part, 256:, :])
            lanes = slice(part * 256, part * 256 + 256)
            for q in range(2):
                row = q * 128
                val[slot, q, :, lanes] = jnp.concatenate(split(s[row : row + 64]), axis=0)
                for side in range(2):
                    w = weight[2 * side + q, pl.ds(c + part, 1), :]
                    rows = slice(side * 128, side * 128 + 128)
                    con[slot, q, rows, lanes] = jnp.concatenate(
                        split(s[row + 64 : row + 128] * w), axis=0
                    )

    def contract(slot):
        for q in range(2):
            acc[q] += dot_t(con[slot, q], val[slot, q])

    def four_groups(t, carry):
        piece(2 * t + 1).wait()
        piece(2 * t + 2).wait()
        spectra(4 * t + 2, 1)
        contract(0)
        spectra(4 * t + 4, 0)
        contract(1)
        return carry

    piece(0).wait()
    spectra(0, 0)
    lax.fori_loop(0, GROUPS // 4 - 1, four_groups, 0)
    piece(GROUPS // 2 - 1).wait()
    spectra(GROUPS - 2, 1)
    contract(0)
    contract(1)

    lane = lax.broadcasted_iota(jnp.int32, (64, 128), 1)
    results = []
    for side in range(2):
        twice = []
        for q in range(2):
            part = acc[q, side * 128 : side * 128 + 64, :]
            part = part + acc[q, side * 128 + 64 : side * 128 + 128, :]
            twice.append(part + pltpu.roll(part, 64, 1))
        high, low = split(blocks_moved(jnp.where(lane < 64, twice[0], twice[1])))
        results.append(dot_t(columns[side], high) + dot_t(columns[side], low))

    first, full = results
    lane = lax.broadcasted_iota(jnp.int32, (128, 128), 1)
    down = pltpu.roll(full, 4, 0)
    even = jnp.where(lane < 64, down, pltpu.roll(full, 64, 1))
    odd = jnp.where(lane < 64, pltpu.roll(down, 64, 1), full)
    first = first.reshape(16, 8, 128)
    for i in range(32):
        out[i // 8, i % 8, :4, :] = first[i // 2, i % 2 * 4 : i % 2 * 4 + 4, :]
    zone = place[0] // 4
    turn = jnp.where(zone == 0, TURNS[0], jnp.where(zone == 3, TURNS[3], 0))
    for i in range(32):
        spot = jnp.bitwise_and(i // 8 + turn, 3)
        value = (even, odd)[i % 2][i // 2 * 8 + 4 : i // 2 * 8 + 8, :]
        out[spot, (i // 2 + 2) % 4 * 2 + i % 2, 4:, :] = value


def make_weight(screen, plane_map, planes, points):
    chosen = screen * (1.0 / (planes * points))
    group = jnp.arange(GROUPS + 1, dtype=jnp.int32)[:, None]
    other = points - plane_map
    direct = (plane_map % OUTER)[None, :] == group
    mirror = ((other % OUTER)[None, :] == group) & (other != plane_map)[None, :]
    mask = jnp.concatenate([direct, mirror], axis=1).astype(F32)
    left = mask[None] * jnp.concatenate([chosen, chosen], axis=1)[:, None, :]
    spot = jnp.concatenate([plane_map // OUTER, other // OUTER])
    right = (spot[None, :] == jnp.arange(INNER, dtype=jnp.int32)[:, None]).astype(F32)
    full = jnp.einsum("qcg,hg->qch", left, right, precision=lax.Precision.HIGHEST)
    even, middle = full[:, 0], full[:, GROUPS, : INNER // 2]
    edge = [even[:, : INNER // 2 + 1], even[:, 1 : INNER // 2], middle, middle]
    rest = full[:, 1:GROUPS]
    rest = jnp.concatenate([rest, rest], axis=2)
    return jnp.concatenate([jnp.concatenate(edge, axis=1)[:, None], rest], axis=1)


VMEM = pl.BlockSpec(memory_space=pltpu.VMEM)
SMEM = pl.BlockSpec(memory_space=pltpu.SMEM)


def call_kernel(
    body, name, *inputs, outs, scalars=0, far=(), scratch=(), limit=16, call=pl.pallas_call
):
    specs = [SMEM] * scalars + [VMEM] * (len(inputs) - scalars)
    inputs = list(inputs)
    for i in far:
        specs[i] = pl.BlockSpec(memory_space=pltpu.HBM)
        inputs[i] = pltpu.with_memory_space_constraint(inputs[i], pltpu.HBM)
    return call(
        body,
        out_shape=outs,
        in_specs=specs,
        out_specs=jax.tree.map(lambda _: VMEM, outs),
        scratch_shapes=scratch,
        compiler_params=pltpu.CompilerParams(vmem_limit_bytes=limit << 20),
        name=name,
    )(*inputs)


def make_turns(call=pl.pallas_call):
    return call_kernel(
        turns_kernel,
        "turns",
        *constants(),
        outs=jax.ShapeDtypeStruct((GROUPS, 512, 256), BF),
        call=call,
    )


def local_blocks(pair, place, data, slab, screens, turns, call=pl.pallas_call):
    return call_kernel(
        block_kernel,
        "pair_blocks",
        pair,
        place,
        data,
        slab,
        screens,
        turns,
        orders(),
        scalars=2,
        outs=jax.ShapeDtypeStruct((4, 8, 8, 128), F32),
        scratch=[
            pltpu.VMEM((OUTER, 48, INNER), F32),
            pltpu.VMEM((GROUPS, 256, 2 * INNER), F32),
            pltpu.VMEM((2, 2, 128, 512), BF),
            pltpu.VMEM((2, 2, 256, 512), BF),
            pltpu.VMEM((2, 256, 128), F32),
            pltpu.VMEM((4, GROUPS, 2 * INNER), F32),
            pltpu.VMEM((2, 128, 128), BF),
            pltpu.VMEM((GROUPS, 512, 256), BF),
            pltpu.SemaphoreType.DMA((GROUPS // 2,)),
        ],
        far=(5,),
        limit=32,
        call=call,
    )


def shards(waves, screen, pair_table, plane_map, trial, probe):
    n_rows = lax.axis_size("ka")
    n_cols = lax.axis_size("kp")
    pair = pair_table.reshape(2)

    out = call_kernel(
        first_kernel,
        "first",
        pair,
        waves.reshape(32, INNER),
        trial.reshape(64, 8).T,
        probe.transpose(0, 2, 1).reshape(8, 64),
        far=range(4),
        outs=jax.ShapeDtypeStruct((n_rows * SLAB, 4, 128), BF),
        scratch=[
            pltpu.SMEM((2,), jnp.int32),
            pltpu.VMEM((32, 128), BF),
            pltpu.VMEM((8, 64), BF),
            pltpu.VMEM((8, 64), BF),
            pltpu.SemaphoreType.DMA((4,)),
        ],
    )
    slab = lax.all_to_all(out, "ka", 0, 0, tiled=True)
    slab, plane_map, screen = lax.optimization_barrier((slab, plane_map, screen))
    out = call_kernel(
        second_kernel,
        "second",
        slab,
        outs=jax.ShapeDtypeStruct((n_cols * BLOCK, 4, 128), BF),
    )
    data = lax.all_to_all(out, "kp", 0, 0, tiled=True)

    place = lax.axis_index("ka").astype(jnp.int32).reshape(1)
    screens = make_weight(screen, plane_map, plane_map.shape[0], OUTER * INNER)
    out = local_blocks(pair, place, data, slab, screens, make_turns())

    parts = lax.all_to_all(out.reshape(n_cols, 8, 128), "kp", 0, 0, tiled=True)
    swap = []
    for a in range(n_rows):
        for b in range(n_rows):
            for c in range(2):
                spot = (b // 4 + TURNS[a // 4]) % 4 * 8 + (b + 2) % 4 * 2 + c
                swap.append((a * n_cols + spot, b * n_cols + 2 * a + c))
    adjoint = lax.ppermute(parts[:, 4:].sum(axis=0), ("ka", "kp"), swap)
    adjoint = call_kernel(last_kernel, "last", adjoint, outs=jax.ShapeDtypeStruct((8, 64), F32))
    applied = parts[:, :4].sum(axis=0).reshape(4, 2, 64)
    return applied.transpose(1, 2, 0), adjoint.T.reshape(1, 64, 8)


def solution(mesh):
    placed = (
        P("ka", None, "kp"),
        P(),
        P("ka", "kp"),
        P(),
        P("kp", None, "ka"),
        P("ka", None, "kp"),
    )
    return jax.shard_map(
        shards,
        mesh=mesh,
        in_specs=placed,
        out_specs=(P("ka", None, "kp"), P("kp", None, "ka")),
        check_vma=False,
    )
```
